512 devices in a mesh: row: 128 (over x, z_hi, y, core), col: 4 (over z_lo).
Axes of the slice: x: 4, y: 4, z: 16 (z_hi: 4, z_lo: 4; z = z_hi * 4 + z_lo), core: 2. Of those that a mesh axis runs over, the one named last changes fastest.
Arguments:
- diag_inverse: float32 [512, 512], replicated, may hold values from -1 to 2, as said below
- panel: float32 [12288, 512], P('row', 'col'), may hold values from -0.3 to 0.3
- trailing: float32 [12288, 12288], P('row', 'col'), may hold values from -6 to 6
- agg_vals: float32 [128, 4, 192, 1024], P('row', 'col'), may hold values from -6 to 6
- agg_dest: int32 [128, 4, 192, 1], P('row', 'col'), may hold values from 0 to 127; in each aligned block of 192 rows (0 to 191, 192 to 383, ..., all dimensions but the last counted through in order) at most 2 rows name the same one
- agg_tile: int32 [128, 4, 192], P('row', 'col'), may hold values from 0 to 287
Outputs:
- updated: float32 [12288, 12288], P('row', 'col')
- panel_factor: float32 [12288, 512], P('row', 'col')
The draws below stay inside these ranges and needn't reach their ends.
Inputs may be any that keep to these rules, and one draw needn't show every extreme that they name: `diag_inverse`: lower triangular with diagonal entries between 0.5 and 2. `agg_dest`: among the aggregates of one device no row index is named more than 2 times, and in some device one is named exactly 2 times.
All inputs are finite; a program needn't handle non-finite values.
Results may differ from the reference program's by a relative error of at most 0.000071.
Values sent between devices are 32-bit elements; how exact they have to be, the bound alone decides.
A program may use at most 64 MiB of HBM per device.

```python
import math
import jax
import jax.numpy as jnp
import numpy as np
from jax import lax

B = 512
TRAIL = 12288
TILE_ROWS = 8
TILE_COLS = 128
CAP = 2
ROWS_DEV = 96
COLS_DEV = 3072
TILES_DEV = 288
AGG = 192
N_ROW = 128
N_COL = 4


def draw_diag_inverse(key, part):
    first_key, second_key = jax.random.split(key)
    diagonal_part = jax.random.uniform(first_key, (B,), jnp.float32, 0.6, 1.6)
    spread_part = jnp.clip(jax.random.normal(second_key, (B, B), jnp.float32), -4.0, 4.0) * (0.7 / math.sqrt(B))
    return jnp.tril(spread_part, -1) + jnp.diag(diagonal_part)


def touch_ends(array, key, smallest, high):
    shape = array.shape
    place = [jax.random.randint(jax.random.fold_in(key, axis), (), 0, shape[axis]) for axis in range(len(shape))]
    array = array.at[tuple(place)].set(smallest)
    longest = shape.index(max(shape))
    place[longest] = (place[longest] + 1) % shape[longest]
    return array.at[tuple(place)].set(high)


def levels(stream_key, dims, pieces, low, largest):
    def one(dim, parts):
        steps = jax.random.uniform(jax.random.fold_in(jax.random.fold_in(stream_key, 6), dim), (parts,), jnp.float32, low / len(pieces), largest / len(pieces))
        return jnp.repeat(jnp.exp(steps), dims[dim] // parts).reshape((-1,) + (1,) * (len(dims) - dim - 1))

    loudness = one(*pieces[0])
    for cut in pieces[1:]:
        loudness = loudness * one(*cut)
    return loudness


def shared_out(rng, own, number, rows, amount, top, bound, slope):
    order = jax.random.permutation(rng, amount)
    packed, usual = load_shares(amount, rows * top, bound, slope, True), load_shares(amount, rows * top, bound, slope, False)
    places = jnp.arange(amount)

    def named(tallies, offset_by):
        used = int((tallies > 0).sum())
        fixed = max(1, used // 4)
        shifted = fixed + (places - fixed + offset_by * (used - fixed)) % max(1, amount - fixed)
        return jnp.zeros((amount,), jnp.int32).at[order[jnp.where(places < fixed, places, shifted)]].set(jnp.asarray(tallies, jnp.int32))

    tallies = jnp.where(number % 4 == 0, named(packed, number // 4), named(usual, number - number // 4 - 1))
    mixed = jax.random.permutation(jax.random.fold_in(own, 3), amount)
    giver, receiver = mixed[0:amount // 2 * 2:2], mixed[1:amount // 2 * 2:2]
    margin = jnp.minimum(tallies[giver] - 1, bound - tallies[receiver]) // 2
    margin = jnp.where((giver == order[0]) | (receiver == order[0]) | (tallies[receiver] == 0), 0, jnp.maximum(margin, 0))
    shifted = jax.random.randint(jax.random.fold_in(own, 4), (amount // 2,), 0, 1 << 20) % (margin + 1)
    tallies = tallies.at[giver].add(-shifted).at[receiver].add(shifted)
    members = jnp.searchsorted(jnp.cumsum(tallies), jnp.arange(rows * top), side="right").astype(jnp.int32)
    grid = members.reshape(top, rows).T
    grid = grid[jax.random.permutation(jax.random.fold_in(own, 1), rows)]
    offset_by = jax.random.randint(jax.random.fold_in(own, 2), (rows, 1), 0, top)
    return jnp.take_along_axis(grid, (jnp.arange(top)[None, :] + offset_by) % top, axis=1)


def load_shares(count, total, reach, skew, full):
    portions = [(1 << 20) // math.isqrt(grade ** skew) + 1 for grade in range(1, count + 1)]
    largest = reach if full else min(reach, max(-(-total // count), total * portions[0] // sum(portions)))
    least = 1 if total - largest >= count - 1 else 0
    counts, surplus = [largest] + [least] * (count - 1), total - largest - least * (count - 1)
    while surplus > 0:
        free = [i for i in range(1, count) if counts[i] < largest] or [i for i in range(1, count) if counts[i] < reach]
        whole, left = sum([portions[i] for i in free]), surplus
        for i in free:
            more = min(reach - counts[i], max(1, left * portions[i] // whole), surplus)
            counts[i] = counts[i] + more
            surplus = surplus - more
    return np.array(counts)


def noise(key, dims, scale, bound, cuts=(), kind=jnp.bfloat16):
    drawn = jax.random.normal(key, dims, jnp.float32) * scale
    if len(cuts) > 0:
        drawn = levels(key, dims, cuts, -0.22, 0.18) * drawn
    return jnp.clip(drawn, min=-bound, max=bound).astype(kind)


def setup_inputs(seed: int = 0) -> dict:
    key_list = jax.random.split(jax.random.key(seed), 7)
    diag_inverse = draw_diag_inverse(jax.random.fold_in(key_list[6], 71), 0)
    panel = noise(key_list[1], (TRAIL, B), 0.05, 0.3, ((0, 128), (1, 4)), jnp.float32)
    trailing = noise(key_list[2], (TRAIL, TRAIL), 1.0, 6.0, ((0, 128), (1, 4)), jnp.float32)
    agg_vals = noise(key_list[3], (N_ROW, N_COL, AGG, TILE_ROWS * TILE_COLS), 1.0, 6.0, ((0, 128), (1, 4)), jnp.float32)
    agg_dest_keys = jax.random.split(jax.random.fold_in(key_list[4], 1), N_ROW * N_COL * AGG // AGG)
    agg_dest_turns = jax.random.permutation(jax.random.fold_in(key_list[4], 3), N_ROW * N_COL * AGG // AGG)
    agg_dest = jax.vmap(lambda own, number: shared_out(jax.random.fold_in(key_list[4], 2), own, number, AGG, N_ROW, 1, CAP, 1))(agg_dest_keys, agg_dest_turns).reshape((N_ROW, N_COL, AGG, 1))
    agg_tile = touch_ends(jax.random.randint(key_list[5], (N_ROW, N_COL, AGG), 0, TILES_DEV), jax.random.fold_in(key_list[5], 1), 0, TILES_DEV - 1).astype(jnp.int32)
    return dict(diag_inverse=diag_inverse, panel=panel, trailing=trailing, agg_vals=agg_vals, agg_dest=agg_dest, agg_tile=agg_tile)


def reference(diag_inverse, panel, trailing, agg_vals, agg_dest, agg_tile):
    panel_factor = jnp.dot(panel, diag_inverse.T, precision=lax.Precision.HIGHEST, preferred_element_type=jnp.float32)
    tile_rows = ROWS_DEV // TILE_ROWS
    tile_cols = COLS_DEV // TILE_COLS
    blocked = trailing.reshape(N_ROW, tile_rows, TILE_ROWS, N_COL, tile_cols, TILE_COLS)
    targets = agg_dest[..., 0].astype(jnp.int32)
    columns = jnp.broadcast_to(jnp.arange(N_COL, dtype=jnp.int32)[None, :, None], targets.shape)
    tile_row_ids = (agg_tile // tile_cols).astype(jnp.int32)
    tile_col_ids = (agg_tile % tile_cols).astype(jnp.int32)
    tiles_in = agg_vals.reshape(N_ROW, N_COL, AGG, TILE_ROWS, TILE_COLS)
    blocked = blocked.at[targets, tile_row_ids, :, columns, tile_col_ids, :].add(tiles_in)
    assembled = blocked.reshape(TRAIL, TRAIL)
    product = jnp.dot(panel_factor, panel_factor.T, precision=lax.Precision.HIGHEST, preferred_element_type=jnp.float32)
    updated = assembled - product
    return updated, panel_factor
```

```python
import jax
import jax.numpy as jnp
import numpy as np
from jax import lax
from jax.sharding import Mesh
from jax.sharding import PartitionSpec as P

TILE_ROWS = 8
TILE_COLS = 128
CAP = 2
ROW_AXES = ("rx", "rin")


def per_device(diag_inverse, panel, trailing, agg_vals, agg_dest, agg_tile):
    row_devices = lax.axis_size(ROW_AXES)
    local_rows, local_cols = trailing.shape
    panel_width = diag_inverse.shape[0]
    part_width = panel_width // lax.axis_size("col")
    col_index = lax.axis_index("col")
    contract_last = (((1,), (1,)), ((), ()))
    panel_whole = lax.all_gather(panel, "col", axis=1, tiled=True)
    own_full = jnp.dot(
        panel_whole,
        diag_inverse.T,
        precision=lax.Precision.HIGHEST,
        preferred_element_type=jnp.float32,
    )
    own_block = lax.dynamic_slice_in_dim(own_full, col_index * part_width, part_width, 1)
    across = lax.all_gather(own_full, "rx", axis=0, tiled=False)
    chosen = lax.dynamic_index_in_dim(across, col_index, 0, keepdims=False)
    partner = lax.all_gather(chosen, "rin", axis=0, tiled=True)
    tile_rows = local_rows // TILE_ROWS
    tile_cols = local_cols // TILE_COLS
    tiles_dev = tile_rows * tile_cols
    tile_values = agg_vals.reshape(agg_vals.shape[2], agg_vals.shape[3])
    targets = agg_dest.reshape(-1)
    tile_ids = agg_tile.reshape(-1)
    matches = (targets[:, None] == jnp.arange(row_devices, dtype=jnp.int32)[None, :]).astype(
        jnp.int32
    )
    earlier = jnp.cumsum(matches, axis=0) - matches
    ranks = jnp.sum(earlier * matches, axis=1)
    position = targets * CAP + ranks
    send_values = (
        jnp.zeros((row_devices * CAP, tile_values.shape[1]), jnp.float32)
        .at[position]
        .set(tile_values)
    )
    send_ids = (
        jnp.full((row_devices * CAP,), float(tiles_dev), jnp.float32)
        .at[position]
        .set(tile_ids.astype(jnp.float32))
    )
    got_values, got_ids = (
        lax.all_to_all(send_values, ROW_AXES, split_axis=0, concat_axis=0, tiled=True),
        lax.all_to_all(send_ids, ROW_AXES, split_axis=0, concat_axis=0, tiled=True),
    )
    landing = got_ids.astype(jnp.int32)
    blocked = trailing.reshape(tile_rows, TILE_ROWS, tile_cols, TILE_COLS)
    blocked = blocked.at[landing // tile_cols, :, landing % tile_cols, :].add(
        got_values.reshape(-1, TILE_ROWS, TILE_COLS), mode="drop"
    )
    assembled = blocked.reshape(local_rows, local_cols)
    product = lax.dot_general(
        own_full,
        partner,
        contract_last,
        precision=lax.Precision.HIGHEST,
        preferred_element_type=jnp.float32,
    )
    updated = assembled - product
    return (updated, own_block)


def solution(mesh):
    n_row, n_col = mesh.devices.shape
    split = Mesh(mesh.devices.reshape(n_col, n_row // n_col, n_col), ROW_AXES + ("col",))
    rows = ROW_AXES
    in_specs = (
        P(),
        P(rows, "col"),
        P(rows, "col"),
        P(rows, "col", None, None),
        P(rows, "col", None, None),
        P(rows, "col", None),
    )
    out_specs = (P(rows, "col"), P(rows, "col"))
    return jax.shard_map(
        per_device, mesh=split, in_specs=in_specs, out_specs=out_specs, check_vma=False
    )
```

```python
import jax
import jax.numpy as jnp
import numpy as np
from jax import lax
from jax.sharding import Mesh
from jax.sharding import PartitionSpec as P

TILE_ROWS = 8
TILE_COLS = 128
CAP = 2
ROW_AXES = ("x", "zh", "y", "core")


def per_device(diag_inverse, panel, trailing, agg_vals, agg_dest, agg_tile):
    row_devices = lax.axis_size(ROW_AXES)
    local_rows, local_cols = trailing.shape
    panel_width = diag_inverse.shape[0]
    part_width = panel_width // lax.axis_size("col")
    col_index = lax.axis_index("col")
    contract_last = (((1,), (1,)), ((), ()))
    panel_whole = lax.all_gather(panel, "col", axis=1, tiled=True)
    own_full = jnp.dot(
        panel_whole,
        diag_inverse.T,
        precision=lax.Precision.HIGHEST,
        preferred_element_type=jnp.float32,
    )
    own_block = lax.dynamic_slice_in_dim(own_full, col_index * part_width, part_width, 1)
    z_quarters = lax.all_gather(own_block, "zh", axis=0, tiled=False)
    z_full = lax.all_gather(z_quarters, "col", axis=2, tiled=True)
    x_index = lax.axis_index("x")
    n_x = lax.axis_size("x")
    n_c = lax.axis_size("col")
    shift = (x_index - col_index) % n_x
    chosen = z_full
    for step in range(1, n_x):
        pairs = [(c * n_c + c, ((c + step) % n_x) * n_c + c) for c in range(n_c)]
        got = lax.ppermute(z_full, ("x", "col"), pairs)
        chosen = jnp.where(shift == step, got, chosen)
    gathered = lax.all_gather(chosen, ("y", "core"), axis=0, tiled=False)
    n_yc = gathered.shape[0]
    n_zh = gathered.shape[1]
    tile_rows = local_rows // TILE_ROWS
    tile_cols = local_cols // TILE_COLS
    tiles_dev = tile_rows * tile_cols
    tile_values = agg_vals.reshape(agg_vals.shape[2], agg_vals.shape[3])
    targets = agg_dest.reshape(-1)
    tile_ids = agg_tile.reshape(-1)
    matches = (targets[:, None] == jnp.arange(row_devices, dtype=jnp.int32)[None, :]).astype(
        jnp.int32
    )
    earlier = jnp.cumsum(matches, axis=0) - matches
    ranks = jnp.sum(earlier * matches, axis=1)
    position = targets * CAP + ranks
    send_values = (
        jnp.zeros((row_devices * CAP, tile_values.shape[1]), jnp.float32)
        .at[position]
        .set(tile_values)
    )
    send_ids = (
        jnp.full((row_devices * CAP,), float(tiles_dev), jnp.float32)
        .at[position]
        .set(tile_ids.astype(jnp.float32))
    )
    got_values, got_ids = (
        lax.all_to_all(send_values, ROW_AXES, split_axis=0, concat_axis=0, tiled=True),
        lax.all_to_all(send_ids, ROW_AXES, split_axis=0, concat_axis=0, tiled=True),
    )
    landing = got_ids.astype(jnp.int32)
    blocked = trailing.reshape(tile_rows, TILE_ROWS, tile_cols, TILE_COLS)
    blocked = blocked.at[landing // tile_cols, :, landing % tile_cols, :].add(
        got_values.reshape(-1, TILE_ROWS, TILE_COLS), mode="drop"
    )
    assembled = blocked.reshape(local_rows, local_cols)
    partner = gathered.reshape(n_yc * n_zh * local_rows, panel_width)
    product = lax.dot_general(
        own_full,
        partner,
        contract_last,
        precision=lax.Precision.HIGHEST,
        preferred_element_type=jnp.float32,
    )
    product = (
        product.reshape(local_rows, n_yc, n_zh, local_rows)
        .transpose(0, 2, 1, 3)
        .reshape(local_rows, local_cols)
    )
    updated = assembled - product
    return (updated, own_block)


def solution(mesh):
    n_row, n_col = mesh.devices.shape
    shape = (n_col, n_col, n_col, n_row // n_col**3, n_col)
    split = Mesh(mesh.devices.reshape(shape), ROW_AXES + ("col",))
    rows = ROW_AXES
    in_specs = (
        P(),
        P(rows, "col"),
        P(rows, "col"),
        P(rows, "col", None, None),
        P(rows, "col", None, None),
        P(rows, "col", None),
    )
    out_specs = (P(rows, "col"), P(rows, "col"))
    return jax.shard_map(
        per_device, mesh=split, in_specs=in_specs, out_specs=out_specs, check_vma=False
    )
```

```python
import jax
import jax.numpy as jnp
from jax import lax
from jax.sharding import Mesh
from jax.sharding import PartitionSpec as P

TILE_ROWS = 8
TILE_COLS = 128
CAP = 2
ROW_AXES = ("x", "zh", "y", "core")


def per_device(diag_inverse, panel, trailing, agg_vals, agg_dest, agg_tile):
    row_devices = lax.axis_size(ROW_AXES)
    local_rows, local_cols = trailing.shape
    panel_width = diag_inverse.shape[0]
    part_width = panel.shape[1]
    col_index = lax.axis_index("col")
    zh_index = lax.axis_index("zh")

    tile_rows = local_rows // TILE_ROWS
    tile_cols = local_cols // TILE_COLS
    tiles_dev = tile_rows * tile_cols
    tile_values = agg_vals.reshape(agg_vals.shape[2], agg_vals.shape[3])
    targets = agg_dest.reshape(-1)
    tile_ids = agg_tile.reshape(-1)
    matches = (targets[:, None] == jnp.arange(row_devices, dtype=jnp.int32)[None, :]).astype(
        jnp.int32
    )
    earlier = jnp.cumsum(matches, axis=0) - matches
    ranks = jnp.sum(earlier * matches, axis=1)
    position = targets * CAP + ranks
    id_lanes = jnp.broadcast_to(tile_ids.astype(jnp.float32)[:, None], (tile_ids.shape[0], TILE_COLS))
    payload = jnp.concatenate([tile_values, id_lanes], axis=1)
    send = (
        jnp.zeros((row_devices * CAP, payload.shape[1]), jnp.float32)
        .at[:, tile_values.shape[1]:]
        .set(float(tiles_dev))
        .at[position]
        .set(payload)
    )
    got = lax.all_to_all(send, ROW_AXES, split_axis=0, concat_axis=0, tiled=True)
    got_values = got[:, : tile_values.shape[1]]
    landing = got[:, tile_values.shape[1]].astype(jnp.int32)

    ring_panel = lax.all_gather(panel, ("zh", "col"), axis=0, tiled=False)
    n_zh = lax.axis_size("zh")
    n_c = lax.axis_size("col")
    ring_panel = ring_panel.reshape(n_zh, n_c, local_rows, part_width)
    ring_panel = ring_panel.transpose(0, 2, 1, 3).reshape(n_zh * local_rows, n_c * part_width)
    ring_factor = jnp.dot(
        ring_panel,
        diag_inverse.T,
        precision=lax.Precision.HIGHEST,
        preferred_element_type=jnp.float32,
    ).reshape(n_zh, local_rows, panel_width)
    own_full = lax.dynamic_index_in_dim(ring_factor, zh_index, 0, keepdims=False)
    own_block = lax.dynamic_slice_in_dim(own_full, col_index * part_width, part_width, 1)

    x_index = lax.axis_index("x")
    n_x = lax.axis_size("x")
    shift = (x_index - col_index) % n_x
    chosen = ring_factor
    for step in range(1, n_x):
        pairs = [(c * n_c + c, ((c + step) % n_x) * n_c + c) for c in range(n_c)]
        moved = lax.ppermute(ring_factor, ("x", "col"), pairs)
        chosen = jnp.where(shift == step, moved, chosen)
    gathered = lax.all_gather(chosen, ("y", "core"), axis=1, tiled=False)
    partner = gathered.reshape(local_cols, panel_width)

    blocked = trailing.reshape(tile_rows, TILE_ROWS, tile_cols, TILE_COLS)
    blocked = blocked.at[landing // tile_cols, :, landing % tile_cols, :].add(
        got_values.reshape(-1, TILE_ROWS, TILE_COLS), mode="drop"
    )
    assembled = blocked.reshape(local_rows, local_cols)
    product = lax.dot_general(
        own_full,
        partner,
        (((1,), (1,)), ((), ())),
        precision=lax.Precision.HIGHEST,
        preferred_element_type=jnp.float32,
    )
    updated = assembled - product
    return (updated, own_block)


def solution(mesh):
    n_row, n_col = mesh.devices.shape
    shape = (n_col, n_col, n_col, n_row // n_col**3, n_col)
    split = Mesh(mesh.devices.reshape(shape), ROW_AXES + ("col",))
    rows = ROW_AXES
    in_specs = (
        P(),
        P(rows, "col"),
        P(rows, "col"),
        P(rows, "col", None, None),
        P(rows, "col", None, None),
        P(rows, "col", None),
    )
    out_specs = (P(rows, "col"), P(rows, "col"))
    return jax.shard_map(
        per_device, mesh=split, in_specs=in_specs, out_specs=out_specs, check_vma=False
    )
```

```python
import functools

import jax
import jax.numpy as jnp
from jax import lax
from jax.experimental import pallas as pl
from jax.experimental.pallas import tpu as pltpu
from jax.sharding import Mesh
from jax.sharding import PartitionSpec as P

TILE_ROWS = 8
TILE_COLS = 128
CAP = 2
ROW_AXES = ("x", "zh", "y", "core")
MESH_IDS = pl.DeviceIdType.MESH


def _ring_gather_kernel(n_zh, n_c, block_ref, out_ref, send_sem, recv_sem):
    n = n_zh * n_c
    me = lax.axis_index("zh") * n_c + lax.axis_index("col")
    right = lax.rem(me + 1, n)
    left = lax.rem(me + n - 1, n)

    def where(p):
        return {"zh": p // n_c, "col": lax.rem(p, n_c)}

    barrier = pltpu.get_barrier_semaphore()
    for other in (left, right):
        pl.semaphore_signal(barrier, 1, device_id=where(other), device_id_type=MESH_IDS)
    pl.semaphore_wait(barrier, 2)
    out_ref[me] = block_ref[...]
    counts = (n // 2, n - 1 - n // 2)
    targets = (right, left)
    signs = (-1, 1)
    sent = ([], [])
    for step in range(max(counts)):
        for d in range(2):
            if step >= counts[d]:
                continue
            slot = lax.rem(me + signs[d] * step + n, n)
            if step > 0:
                sent[d][step - 1].wait_recv()
            src = block_ref if step == 0 else out_ref.at[slot]
            copy = pltpu.make_async_remote_copy(
                src_ref=src,
                dst_ref=out_ref.at[slot],
                send_sem=send_sem.at[d, step],
                recv_sem=recv_sem.at[d, step],
                device_id=where(targets[d]),
                device_id_type=MESH_IDS,
            )
            copy.start()
            sent[d].append(copy)
    for d in range(2):
        if sent[d]:
            sent[d][-1].wait_recv()
        for copy in sent[d]:
            copy.wait_send()


def ring_gather(block, n_zh, n_c):
    n = n_zh * n_c
    steps = max(n // 2, 1)
    return pl.pallas_call(
        functools.partial(_ring_gather_kernel, n_zh, n_c),
        out_shape=jax.ShapeDtypeStruct((n,) + block.shape, block.dtype),
        in_specs=[pl.BlockSpec(memory_space=pltpu.VMEM)],
        out_specs=pl.BlockSpec(memory_space=pltpu.VMEM),
        scratch_shapes=[
            pltpu.SemaphoreType.DMA((2, steps)),
            pltpu.SemaphoreType.DMA((2, steps)),
        ],
        compiler_params=pltpu.CompilerParams(collective_id=0, has_side_effects=True),
    )(block)


def per_device(diag_inverse, panel, trailing, agg_vals, agg_dest, agg_tile):
    row_devices = lax.axis_size(ROW_AXES)
    local_rows, local_cols = trailing.shape
    panel_width = diag_inverse.shape[0]
    part_width = panel.shape[1]
    col_index = lax.axis_index("col")
    zh_index = lax.axis_index("zh")

    tile_rows = local_rows // TILE_ROWS
    tile_cols = local_cols // TILE_COLS
    tiles_dev = tile_rows * tile_cols
    tile_values = agg_vals.reshape(agg_vals.shape[2], agg_vals.shape[3])
    targets = agg_dest.reshape(-1)
    tile_ids = agg_tile.reshape(-1)
    matches = (targets[:, None] == jnp.arange(row_devices, dtype=jnp.int32)[None, :]).astype(
        jnp.int32
    )
    earlier = jnp.cumsum(matches, axis=0) - matches
    ranks = jnp.sum(earlier * matches, axis=1)
    position = targets * CAP + ranks
    id_lanes = jnp.broadcast_to(tile_ids.astype(jnp.float32)[:, None], (tile_ids.shape[0], TILE_COLS))
    payload = jnp.concatenate([tile_values, id_lanes], axis=1)
    send = (
        jnp.zeros((row_devices * CAP, payload.shape[1]), jnp.float32)
        .at[:, tile_values.shape[1]:]
        .set(float(tiles_dev))
        .at[position]
        .set(payload)
    )
    got = lax.all_to_all(send, ROW_AXES, split_axis=0, concat_axis=0, tiled=True)
    got_values = got[:, : tile_values.shape[1]]
    landing = got[:, tile_values.shape[1]].astype(jnp.int32)

    n_zh = lax.axis_size("zh")
    n_c = lax.axis_size("col")
    ring_panel = ring_gather(panel, n_zh, n_c)
    ring_panel = ring_panel.reshape(n_zh, n_c, local_rows, part_width)
    ring_panel = ring_panel.transpose(0, 2, 1, 3).reshape(n_zh * local_rows, n_c * part_width)
    ring_factor = jnp.dot(
        ring_panel,
        diag_inverse.T,
        precision=lax.Precision.HIGHEST,
        preferred_element_type=jnp.float32,
    ).reshape(n_zh, local_rows, panel_width)
    own_full = lax.dynamic_index_in_dim(ring_factor, zh_index, 0, keepdims=False)
    own_block = lax.dynamic_slice_in_dim(own_full, col_index * part_width, part_width, 1)

    x_index = lax.axis_index("x")
    n_x = lax.axis_size("x")
    shift = (x_index - col_index) % n_x
    chosen = ring_factor
    for step in range(1, n_x):
        pairs = [(c * n_c + c, ((c + step) % n_x) * n_c + c) for c in range(n_c)]
        moved = lax.ppermute(ring_factor, ("x", "col"), pairs)
        chosen = jnp.where(shift == step, moved, chosen)
    gathered = lax.all_gather(chosen, ("y", "core"), axis=1, tiled=False)
    partner = gathered.reshape(local_cols, panel_width)

    blocked = trailing.reshape(tile_rows, TILE_ROWS, tile_cols, TILE_COLS)
    blocked = blocked.at[landing // tile_cols, :, landing % tile_cols, :].add(
        got_values.reshape(-1, TILE_ROWS, TILE_COLS), mode="drop"
    )
    assembled = blocked.reshape(local_rows, local_cols)
    product = lax.dot_general(
        own_full,
        partner,
        (((1,), (1,)), ((), ())),
        precision=lax.Precision.HIGHEST,
        preferred_element_type=jnp.float32,
    )
    updated = assembled - product
    return (updated, own_block)


def solution(mesh):
    n_row, n_col = mesh.devices.shape
    shape = (n_col, n_col, n_col, n_row // n_col**3, n_col)
    split = Mesh(mesh.devices.reshape(shape), ROW_AXES + ("col",))
    rows = ROW_AXES
    in_specs = (
        P(),
        P(rows, "col"),
        P(rows, "col"),
        P(rows, "col", None, None),
        P(rows, "col", None, None),
        P(rows, "col", None),
    )
    out_specs = (P(rows, "col"), P(rows, "col"))
    return jax.shard_map(
        per_device, mesh=split, in_specs=in_specs, out_specs=out_specs, check_vma=False
    )
```

```python
import functools

import jax
import jax.numpy as jnp
from jax import lax
from jax.experimental import pallas as pl
from jax.experimental.pallas import tpu as pltpu
from jax.sharding import Mesh
from jax.sharding import PartitionSpec as P

TILE_ROWS = 8
TILE_COLS = 128
CAP = 2
ROW_AXES = ("x", "zh", "y", "core")
MESH_IDS = pl.DeviceIdType.MESH


def _front_kernel(n_x, n_zh, n_c, block_ref, ring_ref, moved_ref, send_sem, recv_sem,
                  xsend_sem, xrecv_sem, local_sem):
    n = n_zh * n_c
    col = lax.axis_index("col")
    x = lax.axis_index("x")
    me = lax.axis_index("zh") * n_c + col
    right = lax.rem(me + 1, n)
    left = lax.rem(me + n - 1, n)
    is_source = x == col

    def on_ring(p):
        return {"zh": p // n_c, "col": lax.rem(p, n_c)}

    def x_peer(k):
        return {"x": lax.rem(x + k, n_x)}

    barrier = pltpu.get_barrier_semaphore()
    for other in (left, right):
        pl.semaphore_signal(barrier, 1, device_id=on_ring(other), device_id_type=MESH_IDS)

    @pl.when(is_source)
    def _():
        for k in range(1, n_x):
            pl.semaphore_signal(barrier, 1, device_id=x_peer(k), device_id_type=MESH_IDS)
        pl.semaphore_wait(barrier, 2 + n_x - 1)

    @pl.when(jnp.logical_not(is_source))
    def _():
        pl.semaphore_signal(barrier, 1, device_id={"x": col}, device_id_type=MESH_IDS)
        pl.semaphore_wait(barrier, 3)

    ring_ref[me] = block_ref[...]

    def x_copy(slot, src, k):
        return pltpu.make_async_remote_copy(
            src_ref=src,
            dst_ref=moved_ref.at[slot],
            send_sem=xsend_sem.at[slot, k - 1],
            recv_sem=xrecv_sem.at[0],
            device_id=x_peer(k),
            device_id_type=MESH_IDS,
        )

    def forward_x(slot, src):
        @pl.when(is_source)
        def _():
            for k in range(1, n_x):
                x_copy(slot, src, k).start()

    forward_x(me, block_ref)
    counts = (n // 2, n - 1 - n // 2)
    targets = (right, left)
    signs = (-1, 1)
    sent = ([], [])
    for step in range(max(counts)):
        for d in range(2):
            if step >= counts[d]:
                continue
            slot = lax.rem(me + signs[d] * step + n, n)
            if step > 0:
                sent[d][step - 1].wait_recv()
                forward_x(slot, ring_ref.at[slot])
            src = block_ref if step == 0 else ring_ref.at[slot]
            copy = pltpu.make_async_remote_copy(
                src_ref=src,
                dst_ref=ring_ref.at[slot],
                send_sem=send_sem.at[d, step],
                recv_sem=recv_sem.at[d, step],
                device_id=on_ring(targets[d]),
                device_id_type=MESH_IDS,
            )
            copy.start()
            sent[d].append(copy)
    for d in range(2):
        if sent[d]:
            sent[d][-1].wait_recv()
            last = lax.rem(me + signs[d] * counts[d] + n, n)
            forward_x(last, ring_ref.at[last])
        for copy in sent[d]:
            copy.wait_send()

    @pl.when(is_source)
    def _():
        for slot in range(n):
            for k in range(1, n_x):
                x_copy(slot, ring_ref.at[slot], k).wait_send()
        local = pltpu.make_async_copy(ring_ref, moved_ref, local_sem.at[0])
        local.start()
        local.wait()

    @pl.when(jnp.logical_not(is_source))
    def _():
        whole = pltpu.make_async_remote_copy(
            src_ref=ring_ref,
            dst_ref=moved_ref,
            send_sem=local_sem.at[0],
            recv_sem=xrecv_sem.at[0],
            device_id={"x": col},
            device_id_type=MESH_IDS,
        )
        whole.wait_recv()


def front_exchange(block, n_x, n_zh, n_c):
    n = n_zh * n_c
    steps = max(n // 2, 1)
    shape = jax.ShapeDtypeStruct((n,) + block.shape, block.dtype)
    return pl.pallas_call(
        functools.partial(_front_kernel, n_x, n_zh, n_c),
        out_shape=(shape, shape),
        in_specs=[pl.BlockSpec(memory_space=pltpu.VMEM)],
        out_specs=(pl.BlockSpec(memory_space=pltpu.VMEM), pl.BlockSpec(memory_space=pltpu.VMEM)),
        scratch_shapes=[
            pltpu.SemaphoreType.DMA((2, steps)),
            pltpu.SemaphoreType.DMA((2, steps)),
            pltpu.SemaphoreType.DMA((n, max(n_x - 1, 1))),
            pltpu.SemaphoreType.DMA((1,)),
            pltpu.SemaphoreType.DMA((1,)),
        ],
        compiler_params=pltpu.CompilerParams(collective_id=0, has_side_effects=True),
    )(block)

def per_device(diag_inverse, panel, trailing, agg_vals, agg_dest, agg_tile):
    row_devices = lax.axis_size(ROW_AXES)
    local_rows, local_cols = trailing.shape
    panel_width = diag_inverse.shape[0]
    part_width = panel.shape[1]
    col_index = lax.axis_index("col")
    zh_index = lax.axis_index("zh")

    tile_rows = local_rows // TILE_ROWS
    tile_cols = local_cols // TILE_COLS
    tiles_dev = tile_rows * tile_cols
    tile_values = agg_vals.reshape(agg_vals.shape[2], agg_vals.shape[3])
    targets = agg_dest.reshape(-1)
    tile_ids = agg_tile.reshape(-1)
    matches = (targets[:, None] == jnp.arange(row_devices, dtype=jnp.int32)[None, :]).astype(
        jnp.int32
    )
    earlier = jnp.cumsum(matches, axis=0) - matches
    ranks = jnp.sum(earlier * matches, axis=1)
    position = targets * CAP + ranks
    id_lanes = jnp.broadcast_to(tile_ids.astype(jnp.float32)[:, None], (tile_ids.shape[0], TILE_COLS))
    payload = jnp.concatenate([tile_values, id_lanes], axis=1)
    send = (
        jnp.zeros((row_devices * CAP, payload.shape[1]), jnp.float32)
        .at[:, tile_values.shape[1]:]
        .set(float(tiles_dev))
        .at[position]
        .set(payload)
    )
    got = lax.all_to_all(send, ROW_AXES, split_axis=0, concat_axis=0, tiled=True)
    got_values = got[:, : tile_values.shape[1]]
    landing = got[:, tile_values.shape[1]].astype(jnp.int32)

    n_zh = lax.axis_size("zh")
    n_c = lax.axis_size("col")
    n_x = lax.axis_size("x")
    ring_panel, moved_panel = front_exchange(panel, n_x, n_zh, n_c)

    def to_rows(blocks):
        blocks = blocks.reshape(n_zh, n_c, local_rows, part_width).transpose(0, 2, 1, 3)
        return blocks.reshape(n_zh * local_rows, n_c * part_width)

    own_panel = lax.dynamic_index_in_dim(
        to_rows(ring_panel).reshape(n_zh, local_rows, panel_width), zh_index, 0, keepdims=False
    )
    own_full = jnp.dot(
        own_panel,
        diag_inverse.T,
        precision=lax.Precision.HIGHEST,
        preferred_element_type=jnp.float32,
    )
    own_block = lax.dynamic_slice_in_dim(own_full, col_index * part_width, part_width, 1)
    chosen = jnp.dot(
        to_rows(moved_panel),
        diag_inverse.T,
        precision=lax.Precision.HIGHEST,
        preferred_element_type=jnp.float32,
    ).reshape(n_zh, local_rows, panel_width)
    gathered = lax.all_gather(chosen, ("y", "core"), axis=1, tiled=False)
    partner = gathered.reshape(local_cols, panel_width)

    blocked = trailing.reshape(tile_rows, TILE_ROWS, tile_cols, TILE_COLS)
    blocked = blocked.at[landing // tile_cols, :, landing % tile_cols, :].add(
        got_values.reshape(-1, TILE_ROWS, TILE_COLS), mode="drop"
    )
    assembled = blocked.reshape(local_rows, local_cols)
    product = lax.dot_general(
        own_full,
        partner,
        (((1,), (1,)), ((), ())),
        precision=lax.Precision.HIGHEST,
        preferred_element_type=jnp.float32,
    )
    updated = assembled - product
    return (updated, own_block)


def solution(mesh):
    n_row, n_col = mesh.devices.shape
    shape = (n_col, n_col, n_col, n_row // n_col**3, n_col)
    split = Mesh(mesh.devices.reshape(shape), ROW_AXES + ("col",))
    rows = ROW_AXES
    in_specs = (
        P(),
        P(rows, "col"),
        P(rows, "col"),
        P(rows, "col", None, None),
        P(rows, "col", None, None),
        P(rows, "col", None),
    )
    out_specs = (P(rows, "col"), P(rows, "col"))
    return jax.shard_map(
        per_device, mesh=split, in_specs=in_specs, out_specs=out_specs, check_vma=False
    )
```

```python
import functools

import jax
import jax.numpy as jnp
from jax import lax
from jax.experimental import pallas as pl
from jax.experimental.pallas import tpu as pltpu
from jax.sharding import Mesh
from jax.sharding import PartitionSpec as P

TILE_ROWS = 8
TILE_COLS = 128
CAP = 2
ROW_AXES = ("x", "zh", "y", "core")
MESH_IDS = pl.DeviceIdType.MESH


def _front_kernel(n_x, n_zh, n_c, block_ref, ring_ref, moved_ref, send_sem, recv_sem,
                  xsend_sem, xrecv_sem, local_sem):
    n = n_zh * n_c
    col = lax.axis_index("col")
    x = lax.axis_index("x")
    me = lax.axis_index("zh") * n_c + col
    right = lax.rem(me + 1, n)
    left = lax.rem(me + n - 1, n)
    is_source = x == col

    def on_ring(p):
        return {"zh": p // n_c, "col": lax.rem(p, n_c)}

    def x_peer(k):
        return {"x": lax.rem(x + k, n_x)}

    barrier = pltpu.get_barrier_semaphore()
    for other in (left, right):
        pl.semaphore_signal(barrier, 1, device_id=on_ring(other), device_id_type=MESH_IDS)

    @pl.when(is_source)
    def _():
        for k in range(1, n_x):
            pl.semaphore_signal(barrier, 1, device_id=x_peer(k), device_id_type=MESH_IDS)
        pl.semaphore_wait(barrier, 2 + n_x - 1)

    @pl.when(jnp.logical_not(is_source))
    def _():
        pl.semaphore_signal(barrier, 1, device_id={"x": col}, device_id_type=MESH_IDS)
        pl.semaphore_wait(barrier, 3)

    ring_ref[me] = block_ref[...]

    def x_copy(slot, src, k):
        return pltpu.make_async_remote_copy(
            src_ref=src,
            dst_ref=moved_ref.at[slot],
            send_sem=xsend_sem.at[slot, k - 1],
            recv_sem=xrecv_sem.at[0],
            device_id=x_peer(k),
            device_id_type=MESH_IDS,
        )

    def forward_x(slot, src):
        @pl.when(is_source)
        def _():
            for k in range(1, n_x):
                x_copy(slot, src, k).start()

    forward_x(me, block_ref)
    counts = (n // 2, n - 1 - n // 2)
    targets = (right, left)
    signs = (-1, 1)
    sent = ([], [])
    for step in range(max(counts)):
        for d in range(2):
            if step >= counts[d]:
                continue
            slot = lax.rem(me + signs[d] * step + n, n)
            if step > 0:
                sent[d][step - 1].wait_recv()
                forward_x(slot, ring_ref.at[slot])
            src = block_ref if step == 0 else ring_ref.at[slot]
            copy = pltpu.make_async_remote_copy(
                src_ref=src,
                dst_ref=ring_ref.at[slot],
                send_sem=send_sem.at[d, step],
                recv_sem=recv_sem.at[d, step],
                device_id=on_ring(targets[d]),
                device_id_type=MESH_IDS,
            )
            copy.start()
            sent[d].append(copy)
    for d in range(2):
        if sent[d]:
            sent[d][-1].wait_recv()
            last = lax.rem(me + signs[d] * counts[d] + n, n)
            forward_x(last, ring_ref.at[last])
        for copy in sent[d]:
            copy.wait_send()

    @pl.when(is_source)
    def _():
        for slot in range(n):
            for k in range(1, n_x):
                x_copy(slot, ring_ref.at[slot], k).wait_send()
        local = pltpu.make_async_copy(ring_ref, moved_ref, local_sem.at[0])
        local.start()
        local.wait()

    @pl.when(jnp.logical_not(is_source))
    def _():
        whole = pltpu.make_async_remote_copy(
            src_ref=ring_ref,
            dst_ref=moved_ref,
            send_sem=local_sem.at[0],
            recv_sem=xrecv_sem.at[0],
            device_id={"x": col},
            device_id_type=MESH_IDS,
        )
        whole.wait_recv()


def front_exchange(block, n_x, n_zh, n_c):
    n = n_zh * n_c
    steps = max(n // 2, 1)
    shape = jax.ShapeDtypeStruct((n,) + block.shape, block.dtype)
    return pl.pallas_call(
        functools.partial(_front_kernel, n_x, n_zh, n_c),
        out_shape=(shape, shape),
        in_specs=[pl.BlockSpec(memory_space=pltpu.VMEM)],
        out_specs=(pl.BlockSpec(memory_space=pltpu.VMEM), pl.BlockSpec(memory_space=pltpu.VMEM)),
        scratch_shapes=[
            pltpu.SemaphoreType.DMA((2, steps)),
            pltpu.SemaphoreType.DMA((2, steps)),
            pltpu.SemaphoreType.DMA((n, max(n_x - 1, 1))),
            pltpu.SemaphoreType.DMA((1,)),
            pltpu.SemaphoreType.DMA((1,)),
        ],
        compiler_params=pltpu.CompilerParams(collective_id=0, has_side_effects=True),
    )(block)


def _exchange_kernel(sizes, send_ref, recv_ref, send_sem, recv_sem, local_sem):
    n = 1
    me = 0
    for axis, size in zip(ROW_AXES, sizes):
        me = me * size + lax.axis_index(axis)
        n *= size

    def where(d):
        place = {}
        for axis, size in reversed(list(zip(ROW_AXES, sizes))):
            place[axis] = lax.rem(d, size)
            d = d // size
        return place

    local = pltpu.make_async_copy(send_ref.at[me], recv_ref.at[me], local_sem.at[0])
    local.start()

    def body(k, carry):
        d = lax.rem(me + k, n)
        pltpu.make_async_remote_copy(
            src_ref=send_ref.at[d],
            dst_ref=recv_ref.at[me],
            send_sem=send_sem.at[0],
            recv_sem=recv_sem.at[0],
            device_id=where(d),
            device_id_type=MESH_IDS,
        ).start()
        return carry

    lax.fori_loop(1, n, body, 0)
    every = pltpu.make_async_remote_copy(
        src_ref=send_ref.at[pl.ds(0, n - 1)],
        dst_ref=recv_ref.at[pl.ds(0, n - 1)],
        send_sem=send_sem.at[0],
        recv_sem=recv_sem.at[0],
        device_id=where(lax.rem(me + 1, n)),
        device_id_type=MESH_IDS,
    )
    every.wait_send()
    every.wait_recv()
    local.wait()


def row_exchange(send, sizes):
    return pl.pallas_call(
        functools.partial(_exchange_kernel, sizes),
        out_shape=jax.ShapeDtypeStruct(send.shape, send.dtype),
        in_specs=[pl.BlockSpec(memory_space=pl.ANY)],
        out_specs=pl.BlockSpec(memory_space=pl.ANY),
        scratch_shapes=[
            pltpu.SemaphoreType.DMA((1,)),
            pltpu.SemaphoreType.DMA((1,)),
            pltpu.SemaphoreType.DMA((1,)),
        ],
        compiler_params=pltpu.CompilerParams(has_side_effects=True),
    )(send)

def per_device(diag_inverse, panel, trailing, agg_vals, agg_dest, agg_tile):
    row_devices = lax.axis_size(ROW_AXES)
    local_rows, local_cols = trailing.shape
    panel_width = diag_inverse.shape[0]
    part_width = panel.shape[1]
    col_index = lax.axis_index("col")
    zh_index = lax.axis_index("zh")

    tile_rows = local_rows // TILE_ROWS
    tile_cols = local_cols // TILE_COLS
    tiles_dev = tile_rows * tile_cols
    tile_values = agg_vals.reshape(agg_vals.shape[2], agg_vals.shape[3])
    targets = agg_dest.reshape(-1)
    tile_ids = agg_tile.reshape(-1)
    matches = (targets[:, None] == jnp.arange(row_devices, dtype=jnp.int32)[None, :]).astype(
        jnp.int32
    )
    earlier = jnp.cumsum(matches, axis=0) - matches
    ranks = jnp.sum(earlier * matches, axis=1)
    position = targets * CAP + ranks
    id_lanes = jnp.broadcast_to(tile_ids.astype(jnp.float32)[:, None], (tile_ids.shape[0], TILE_COLS))
    payload = jnp.concatenate([tile_values, id_lanes], axis=1)
    send = (
        jnp.zeros((row_devices * CAP, payload.shape[1]), jnp.float32)
        .at[:, tile_values.shape[1]:]
        .set(float(tiles_dev))
        .at[position]
        .set(payload)
    )
    row_sizes = tuple(lax.axis_size(axis) for axis in ROW_AXES)
    slabs = send.reshape(row_devices, CAP * payload.shape[1] // TILE_COLS, TILE_COLS)
    got = row_exchange(slabs, row_sizes).reshape(send.shape)
    got_values = got[:, : tile_values.shape[1]]
    landing = got[:, tile_values.shape[1]].astype(jnp.int32)

    n_zh = lax.axis_size("zh")
    n_c = lax.axis_size("col")
    n_x = lax.axis_size("x")
    ring_panel, moved_panel = front_exchange(panel, n_x, n_zh, n_c)

    def to_rows(blocks):
        blocks = blocks.reshape(n_zh, n_c, local_rows, part_width).transpose(0, 2, 1, 3)
        return blocks.reshape(n_zh * local_rows, n_c * part_width)

    own_panel = lax.dynamic_index_in_dim(
        to_rows(ring_panel).reshape(n_zh, local_rows, panel_width), zh_index, 0, keepdims=False
    )
    own_full = jnp.dot(
        own_panel,
        diag_inverse.T,
        precision=lax.Precision.HIGHEST,
        preferred_element_type=jnp.float32,
    )
    own_block = lax.dynamic_slice_in_dim(own_full, col_index * part_width, part_width, 1)
    chosen = jnp.dot(
        to_rows(moved_panel),
        diag_inverse.T,
        precision=lax.Precision.HIGHEST,
        preferred_element_type=jnp.float32,
    ).reshape(n_zh, local_rows, panel_width)
    gathered = lax.all_gather(chosen, ("y", "core"), axis=1, tiled=False)
    partner = gathered.reshape(local_cols, panel_width)

    blocked = trailing.reshape(tile_rows, TILE_ROWS, tile_cols, TILE_COLS)
    blocked = blocked.at[landing // tile_cols, :, landing % tile_cols, :].add(
        got_values.reshape(-1, TILE_ROWS, TILE_COLS), mode="drop"
    )
    assembled = blocked.reshape(local_rows, local_cols)
    product = lax.dot_general(
        own_full,
        partner,
        (((1,), (1,)), ((), ())),
        precision=lax.Precision.HIGHEST,
        preferred_element_type=jnp.float32,
    )
    updated = assembled - product
    return (updated, own_block)


def solution(mesh):
    n_row, n_col = mesh.devices.shape
    shape = (n_col, n_col, n_col, n_row // n_col**3, n_col)
    split = Mesh(mesh.devices.reshape(shape), ROW_AXES + ("col",))
    rows = ROW_AXES
    in_specs = (
        P(),
        P(rows, "col"),
        P(rows, "col"),
        P(rows, "col", None, None),
        P(rows, "col", None, None),
        P(rows, "col", None),
    )
    out_specs = (P(rows, "col"), P(rows, "col"))
    return jax.shard_map(
        per_device, mesh=split, in_specs=in_specs, out_specs=out_specs, check_vma=False
    )
```

```python
import functools

import jax
import jax.numpy as jnp
from jax import lax
from jax.experimental import pallas as pl
from jax.experimental.pallas import tpu as pltpu
from jax.sharding import Mesh
from jax.sharding import PartitionSpec as P

TILE_ROWS = 8
TILE_COLS = 128
CAP = 2
ROW_AXES = ("x", "zh", "y", "core")
MESH_IDS = pl.DeviceIdType.MESH


def _front_kernel(n_x, n_zh, n_c, sizes, block_ref, slab_ref, ring_ref, moved_ref, got_ref,
                  send_sem, recv_sem, xsend_sem, xrecv_sem, local_sem, agg_sem):
    n = n_zh * n_c
    col = lax.axis_index("col")
    x = lax.axis_index("x")
    me = lax.axis_index("zh") * n_c + col
    right = lax.rem(me + 1, n)
    left = lax.rem(me + n - 1, n)
    is_source = x == col

    def on_ring(p):
        return {"zh": p // n_c, "col": lax.rem(p, n_c)}

    def x_peer(k):
        return {"x": lax.rem(x + k, n_x)}

    n_rows = 1
    row_me = 0
    for axis, size in zip(ROW_AXES, sizes):
        row_me = row_me * size + lax.axis_index(axis)
        n_rows *= size

    def on_row(d):
        place = {}
        for axis, size in reversed(list(zip(ROW_AXES, sizes))):
            place[axis] = lax.rem(d, size)
            d = d // size
        return place

    barrier = pltpu.get_barrier_semaphore()
    for other in (left, right):
        pl.semaphore_signal(barrier, 1, device_id=on_ring(other), device_id_type=MESH_IDS)

    def greet(k, carry):
        d = lax.rem(row_me + k, n_rows)
        pl.semaphore_signal(barrier, 1, device_id=on_row(d), device_id_type=MESH_IDS)
        return carry

    lax.fori_loop(1, n_rows, greet, 0)

    @pl.when(is_source)
    def _():
        for k in range(1, n_x):
            pl.semaphore_signal(barrier, 1, device_id=x_peer(k), device_id_type=MESH_IDS)
        pl.semaphore_wait(barrier, 2 + n_x - 1 + n_rows - 1)

    @pl.when(jnp.logical_not(is_source))
    def _():
        pl.semaphore_signal(barrier, 1, device_id={"x": col}, device_id_type=MESH_IDS)
        pl.semaphore_wait(barrier, 3 + n_rows - 1)

    own_slab = pltpu.make_async_copy(slab_ref.at[row_me], got_ref.at[row_me], local_sem.at[1])
    own_slab.start()

    def post(k, carry):
        d = lax.rem(row_me + k, n_rows)
        pltpu.make_async_remote_copy(
            src_ref=slab_ref.at[d],
            dst_ref=got_ref.at[row_me],
            send_sem=agg_sem.at[0],
            recv_sem=agg_sem.at[1],
            device_id=on_row(d),
            device_id_type=MESH_IDS,
        ).start()
        return carry

    lax.fori_loop(1, n_rows, post, 0)

    ring_ref[me] = block_ref[...]

    def x_copy(slot, src, k):
        return pltpu.make_async_remote_copy(
            src_ref=src,
            dst_ref=moved_ref.at[slot],
            send_sem=xsend_sem.at[slot, k - 1],
            recv_sem=xrecv_sem.at[0],
            device_id=x_peer(k),
            device_id_type=MESH_IDS,
        )

    def forward_x(slot, src):
        @pl.when(is_source)
        def _():
            for k in range(1, n_x):
                x_copy(slot, src, k).start()

    forward_x(me, block_ref)
    counts = (n // 2, n - 1 - n // 2)
    targets = (right, left)
    signs = (-1, 1)
    sent = ([], [])
    for step in range(max(counts)):
        for d in range(2):
            if step >= counts[d]:
                continue
            slot = lax.rem(me + signs[d] * step + n, n)
            if step > 0:
                sent[d][step - 1].wait_recv()
                forward_x(slot, ring_ref.at[slot])
            src = block_ref if step == 0 else ring_ref.at[slot]
            copy = pltpu.make_async_remote_copy(
                src_ref=src,
                dst_ref=ring_ref.at[slot],
                send_sem=send_sem.at[d, step],
                recv_sem=recv_sem.at[d, step],
                device_id=on_ring(targets[d]),
                device_id_type=MESH_IDS,
            )
            copy.start()
            sent[d].append(copy)
    for d in range(2):
        if sent[d]:
            sent[d][-1].wait_recv()
            last = lax.rem(me + signs[d] * counts[d] + n, n)
            forward_x(last, ring_ref.at[last])
        for copy in sent[d]:
            copy.wait_send()

    @pl.when(is_source)
    def _():
        for slot in range(n):
            for k in range(1, n_x):
                x_copy(slot, ring_ref.at[slot], k).wait_send()
        local = pltpu.make_async_copy(ring_ref, moved_ref, local_sem.at[0])
        local.start()
        local.wait()

    @pl.when(jnp.logical_not(is_source))
    def _():
        whole = pltpu.make_async_remote_copy(
            src_ref=ring_ref,
            dst_ref=moved_ref,
            send_sem=local_sem.at[0],
            recv_sem=xrecv_sem.at[0],
            device_id={"x": col},
            device_id_type=MESH_IDS,
        )
        whole.wait_recv()

    every = pltpu.make_async_remote_copy(
        src_ref=slab_ref.at[pl.ds(0, n_rows - 1)],
        dst_ref=got_ref.at[pl.ds(0, n_rows - 1)],
        send_sem=agg_sem.at[0],
        recv_sem=agg_sem.at[1],
        device_id=on_row(lax.rem(row_me + 1, n_rows)),
        device_id_type=MESH_IDS,
    )
    every.wait_send()
    every.wait_recv()
    own_slab.wait()


def front_exchange(block, slabs, n_x, n_zh, n_c, sizes):
    n = n_zh * n_c
    steps = max(n // 2, 1)
    shape = jax.ShapeDtypeStruct((n,) + block.shape, block.dtype)
    vmem = pl.BlockSpec(memory_space=pltpu.VMEM)
    anywhere = pl.BlockSpec(memory_space=pl.ANY)
    return pl.pallas_call(
        functools.partial(_front_kernel, n_x, n_zh, n_c, sizes),
        out_shape=(shape, shape, jax.ShapeDtypeStruct(slabs.shape, slabs.dtype)),
        in_specs=[vmem, anywhere],
        out_specs=(vmem, vmem, anywhere),
        scratch_shapes=[
            pltpu.SemaphoreType.DMA((2, steps)),
            pltpu.SemaphoreType.DMA((2, steps)),
            pltpu.SemaphoreType.DMA((n, max(n_x - 1, 1))),
            pltpu.SemaphoreType.DMA((1,)),
            pltpu.SemaphoreType.DMA((2,)),
            pltpu.SemaphoreType.DMA((2,)),
        ],
        compiler_params=pltpu.CompilerParams(collective_id=0, has_side_effects=True),
    )(block, slabs)


def per_device(diag_inverse, panel, trailing, agg_vals, agg_dest, agg_tile):
    row_devices = lax.axis_size(ROW_AXES)
    local_rows, local_cols = trailing.shape
    panel_width = diag_inverse.shape[0]
    part_width = panel.shape[1]
    col_index = lax.axis_index("col")
    zh_index = lax.axis_index("zh")

    tile_rows = local_rows // TILE_ROWS
    tile_cols = local_cols // TILE_COLS
    tiles_dev = tile_rows * tile_cols
    tile_values = agg_vals.reshape(agg_vals.shape[2], agg_vals.shape[3])
    targets = agg_dest.reshape(-1)
    tile_ids = agg_tile.reshape(-1)
    matches = (targets[:, None] == jnp.arange(row_devices, dtype=jnp.int32)[None, :]).astype(
        jnp.int32
    )
    earlier = jnp.cumsum(matches, axis=0) - matches
    ranks = jnp.sum(earlier * matches, axis=1)
    position = targets * CAP + ranks
    id_lanes = jnp.broadcast_to(tile_ids.astype(jnp.float32)[:, None], (tile_ids.shape[0], TILE_COLS))
    payload = jnp.concatenate([tile_values, id_lanes], axis=1)
    send = (
        jnp.zeros((row_devices * CAP, payload.shape[1]), jnp.float32)
        .at[:, tile_values.shape[1]:]
        .set(float(tiles_dev))
        .at[position]
        .set(payload)
    )
    row_sizes = tuple(lax.axis_size(axis) for axis in ROW_AXES)
    slabs = send.reshape(row_devices, CAP * payload.shape[1] // TILE_COLS, TILE_COLS)

    n_zh = lax.axis_size("zh")
    n_c = lax.axis_size("col")
    n_x = lax.axis_size("x")
    ring_panel, moved_panel, got = front_exchange(panel, slabs, n_x, n_zh, n_c, row_sizes)
    got = got.reshape(send.shape)
    got_values = got[:, : tile_values.shape[1]]
    landing = got[:, tile_values.shape[1]].astype(jnp.int32)

    def to_rows(blocks):
        blocks = blocks.reshape(n_zh, n_c, local_rows, part_width).transpose(0, 2, 1, 3)
        return blocks.reshape(n_zh * local_rows, n_c * part_width)

    own_panel = lax.dynamic_index_in_dim(
        to_rows(ring_panel).reshape(n_zh, local_rows, panel_width), zh_index, 0, keepdims=False
    )
    own_full = jnp.dot(
        own_panel,
        diag_inverse.T,
        precision=lax.Precision.HIGHEST,
        preferred_element_type=jnp.float32,
    )
    own_block = lax.dynamic_slice_in_dim(own_full, col_index * part_width, part_width, 1)
    chosen = jnp.dot(
        to_rows(moved_panel),
        diag_inverse.T,
        precision=lax.Precision.HIGHEST,
        preferred_element_type=jnp.float32,
    ).reshape(n_zh, local_rows, panel_width)
    gathered = lax.all_gather(chosen, ("y", "core"), axis=1, tiled=False)
    partner = gathered.reshape(local_cols, panel_width)

    blocked = trailing.reshape(tile_rows, TILE_ROWS, tile_cols, TILE_COLS)
    blocked = blocked.at[landing // tile_cols, :, landing % tile_cols, :].add(
        got_values.reshape(-1, TILE_ROWS, TILE_COLS), mode="drop"
    )
    assembled = blocked.reshape(local_rows, local_cols)
    product = lax.dot_general(
        own_full,
        partner,
        (((1,), (1,)), ((), ())),
        precision=lax.Precision.HIGHEST,
        preferred_element_type=jnp.float32,
    )
    updated = assembled - product
    return (updated, own_block)


def solution(mesh):
    n_row, n_col = mesh.devices.shape
    shape = (n_col, n_col, n_col, n_row // n_col**3, n_col)
    split = Mesh(mesh.devices.reshape(shape), ROW_AXES + ("col",))
    rows = ROW_AXES
    in_specs = (
        P(),
        P(rows, "col"),
        P(rows, "col"),
        P(rows, "col", None, None),
        P(rows, "col", None, None),
        P(rows, "col", None),
    )
    out_specs = (P(rows, "col"), P(rows, "col"))
    return jax.shard_map(
        per_device, mesh=split, in_specs=in_specs, out_specs=out_specs, check_vma=False
    )
```

```python
import functools

import jax
import jax.numpy as jnp
from jax import lax
from jax.experimental import pallas as pl
from jax.experimental.pallas import tpu as pltpu
from jax.sharding import Mesh
from jax.sharding import PartitionSpec as P

TILE_ROWS = 8
TILE_COLS = 128
CAP = 2
ROW_AXES = ("x", "zh", "y", "core")
MESH_IDS = pl.DeviceIdType.MESH


def _front_kernel(n_x, n_zh, n_c, block_ref, ring_ref, moved_ref, send_sem, recv_sem,
                  xsend_sem, xrecv_sem, local_sem):
    n = n_zh * n_c
    col = lax.axis_index("col")
    x = lax.axis_index("x")
    me = lax.axis_index("zh") * n_c + col
    right = lax.rem(me + 1, n)
    left = lax.rem(me + n - 1, n)
    is_source = x == col

    def on_ring(p):
        return {"zh": p // n_c, "col": lax.rem(p, n_c)}

    def x_peer(k):
        return {"x": lax.rem(x + k, n_x)}

    barrier = pltpu.get_barrier_semaphore()
    for other in (left, right):
        pl.semaphore_signal(barrier, 1, device_id=on_ring(other), device_id_type=MESH_IDS)

    @pl.when(is_source)
    def _():
        for k in range(1, n_x):
            pl.semaphore_signal(barrier, 1, device_id=x_peer(k), device_id_type=MESH_IDS)
        pl.semaphore_wait(barrier, 2 + n_x - 1)

    @pl.when(jnp.logical_not(is_source))
    def _():
        pl.semaphore_signal(barrier, 1, device_id={"x": col}, device_id_type=MESH_IDS)
        pl.semaphore_wait(barrier, 3)

    ring_ref[me] = block_ref[...]

    def x_copy(slot, src, k):
        return pltpu.make_async_remote_copy(
            src_ref=src,
            dst_ref=moved_ref.at[slot],
            send_sem=xsend_sem.at[slot, k - 1],
            recv_sem=xrecv_sem.at[0],
            device_id=x_peer(k),
            device_id_type=MESH_IDS,
        )

    def forward_x(slot, src):
        @pl.when(is_source)
        def _():
            for k in range(1, n_x):
                x_copy(slot, src, k).start()

    forward_x(me, block_ref)
    counts = (n // 2, n - 1 - n // 2)
    targets = (right, left)
    signs = (-1, 1)
    sent = ([], [])
    for step in range(max(counts)):
        for d in range(2):
            if step >= counts[d]:
                continue
            slot = lax.rem(me + signs[d] * step + n, n)
            if step > 0:
                sent[d][step - 1].wait_recv()
                forward_x(slot, ring_ref.at[slot])
            src = block_ref if step == 0 else ring_ref.at[slot]
            copy = pltpu.make_async_remote_copy(
                src_ref=src,
                dst_ref=ring_ref.at[slot],
                send_sem=send_sem.at[d, step],
                recv_sem=recv_sem.at[d, step],
                device_id=on_ring(targets[d]),
                device_id_type=MESH_IDS,
            )
            copy.start()
            sent[d].append(copy)
    for d in range(2):
        if sent[d]:
            sent[d][-1].wait_recv()
            last = lax.rem(me + signs[d] * counts[d] + n, n)
            forward_x(last, ring_ref.at[last])
        for copy in sent[d]:
            copy.wait_send()

    @pl.when(is_source)
    def _():
        for slot in range(n):
            for k in range(1, n_x):
                x_copy(slot, ring_ref.at[slot], k).wait_send()
        local = pltpu.make_async_copy(ring_ref, moved_ref, local_sem.at[0])
        local.start()
        local.wait()

    @pl.when(jnp.logical_not(is_source))
    def _():
        whole = pltpu.make_async_remote_copy(
            src_ref=ring_ref,
            dst_ref=moved_ref,
            send_sem=local_sem.at[0],
            recv_sem=xrecv_sem.at[0],
            device_id={"x": col},
            device_id_type=MESH_IDS,
        )
        whole.wait_recv()


def front_exchange(block, n_x, n_zh, n_c):
    n = n_zh * n_c
    steps = max(n // 2, 1)
    shape = jax.ShapeDtypeStruct((n,) + block.shape, block.dtype)
    return pl.pallas_call(
        functools.partial(_front_kernel, n_x, n_zh, n_c),
        out_shape=(shape, shape),
        in_specs=[pl.BlockSpec(memory_space=pltpu.VMEM)],
        out_specs=(pl.BlockSpec(memory_space=pltpu.VMEM), pl.BlockSpec(memory_space=pltpu.VMEM)),
        scratch_shapes=[
            pltpu.SemaphoreType.DMA((2, steps)),
            pltpu.SemaphoreType.DMA((2, steps)),
            pltpu.SemaphoreType.DMA((n, max(n_x - 1, 1))),
            pltpu.SemaphoreType.DMA((1,)),
            pltpu.SemaphoreType.DMA((1,)),
        ],
        compiler_params=pltpu.CompilerParams(collective_id=0, has_side_effects=True),
    )(block)

def per_device(diag_inverse, panel, trailing, agg_vals, agg_dest, agg_tile):
    row_devices = lax.axis_size(ROW_AXES)
    local_rows, local_cols = trailing.shape
    panel_width = diag_inverse.shape[0]
    part_width = panel.shape[1]
    col_index = lax.axis_index("col")
    zh_index = lax.axis_index("zh")

    tile_rows = local_rows // TILE_ROWS
    tile_cols = local_cols // TILE_COLS
    tiles_dev = tile_rows * tile_cols
    tile_values = agg_vals.reshape(agg_vals.shape[2], agg_vals.shape[3])
    targets = agg_dest.reshape(-1)
    tile_ids = agg_tile.reshape(-1)
    matches = (targets[:, None] == jnp.arange(row_devices, dtype=jnp.int32)[None, :]).astype(
        jnp.int32
    )
    earlier = jnp.cumsum(matches, axis=0) - matches
    ranks = jnp.sum(earlier * matches, axis=1)
    position = targets * CAP + ranks
    id_lanes = jnp.broadcast_to(tile_ids.astype(jnp.float32)[:, None], (tile_ids.shape[0], TILE_COLS))
    payload = jnp.concatenate([tile_values, id_lanes], axis=1)
    send = (
        jnp.zeros((row_devices * CAP, payload.shape[1]), jnp.float32)
        .at[:, tile_values.shape[1]:]
        .set(float(tiles_dev))
        .at[position]
        .set(payload)
    )
    got = lax.all_to_all(send, ROW_AXES, split_axis=0, concat_axis=0, tiled=True)
    got_values = got[:, : tile_values.shape[1]]
    landing = got[:, tile_values.shape[1]].astype(jnp.int32)

    n_zh = lax.axis_size("zh")
    n_c = lax.axis_size("col")
    n_x = lax.axis_size("x")
    ring_panel, moved_panel = front_exchange(panel, n_x, n_zh, n_c)

    def to_rows(blocks):
        blocks = blocks.reshape(n_zh, n_c, local_rows, part_width).transpose(0, 2, 1, 3)
        return blocks.reshape(n_zh * local_rows, n_c * part_width)

    own_panel = lax.dynamic_index_in_dim(
        to_rows(ring_panel).reshape(n_zh, local_rows, panel_width), zh_index, 0, keepdims=False
    )
    own_full = jnp.dot(
        own_panel,
        diag_inverse.T,
        precision=lax.Precision.HIGHEST,
        preferred_element_type=jnp.float32,
    )
    own_block = lax.dynamic_slice_in_dim(own_full, col_index * part_width, part_width, 1)
    chosen = jnp.dot(
        to_rows(moved_panel),
        diag_inverse.T,
        precision=lax.Precision.HIGHEST,
        preferred_element_type=jnp.float32,
    ).reshape(n_zh, local_rows, panel_width)
    gathered = lax.all_gather(chosen, ("y", "core"), axis=1, tiled=False)
    partner = gathered.reshape(local_cols, panel_width)

    product = lax.dot_general(
        own_full,
        partner,
        (((1,), (1,)), ((), ())),
        precision=lax.Precision.HIGH,
        preferred_element_type=jnp.float32,
    )
    reduced = (trailing - product).reshape(tile_rows, TILE_ROWS, tile_cols, TILE_COLS)
    reduced = reduced.at[landing // tile_cols, :, landing % tile_cols, :].add(
        got_values.reshape(-1, TILE_ROWS, TILE_COLS), mode="drop"
    )
    updated = reduced.reshape(local_rows, local_cols)
    return (updated, own_block)


def solution(mesh):
    n_row, n_col = mesh.devices.shape
    shape = (n_col, n_col, n_col, n_row // n_col**3, n_col)
    split = Mesh(mesh.devices.reshape(shape), ROW_AXES + ("col",))
    rows = ROW_AXES
    in_specs = (
        P(),
        P(rows, "col"),
        P(rows, "col"),
        P(rows, "col", None, None),
        P(rows, "col", None, None),
        P(rows, "col", None),
    )
    out_specs = (P(rows, "col"), P(rows, "col"))
    return jax.shard_map(
        per_device, mesh=split, in_specs=in_specs, out_specs=out_specs, check_vma=False
    )
```

```python
import functools

import jax
import jax.numpy as jnp
from jax import lax
from jax.experimental import pallas as pl
from jax.experimental.pallas import tpu as pltpu
from jax.sharding import Mesh
from jax.sharding import PartitionSpec as P

TILE_ROWS = 8
TILE_COLS = 128
CAP = 2
ROW_AXES = ("x", "zh", "y", "core")
MESH_IDS = pl.DeviceIdType.MESH


def _front_kernel(n_x, n_zh, n_c, block_ref, ring_ref, moved_ref, send_sem, recv_sem,
                  xsend_sem, xrecv_sem, local_sem):
    n = n_zh * n_c
    col = lax.axis_index("col")
    x = lax.axis_index("x")
    me = lax.axis_index("zh") * n_c + col
    right = lax.rem(me + 1, n)
    left = lax.rem(me + n - 1, n)
    is_source = x == col

    def on_ring(p):
        return {"zh": p // n_c, "col": lax.rem(p, n_c)}

    def x_peer(k):
        return {"x": lax.rem(x + k, n_x)}

    barrier = pltpu.get_barrier_semaphore()
    for other in (left, right):
        pl.semaphore_signal(barrier, 1, device_id=on_ring(other), device_id_type=MESH_IDS)

    @pl.when(is_source)
    def _():
        for k in range(1, n_x):
            pl.semaphore_signal(barrier, 1, device_id=x_peer(k), device_id_type=MESH_IDS)
        pl.semaphore_wait(barrier, 2 + n_x - 1)

    @pl.when(jnp.logical_not(is_source))
    def _():
        pl.semaphore_signal(barrier, 1, device_id={"x": col}, device_id_type=MESH_IDS)
        pl.semaphore_wait(barrier, 3)

    ring_ref[me] = block_ref[...]

    def x_copy(slot, src, k):
        return pltpu.make_async_remote_copy(
            src_ref=src,
            dst_ref=moved_ref.at[slot],
            send_sem=xsend_sem.at[slot, k - 1],
            recv_sem=xrecv_sem.at[0],
            device_id=x_peer(k),
            device_id_type=MESH_IDS,
        )

    def forward_x(slot, src):
        @pl.when(is_source)
        def _():
            for k in range(1, n_x):
                x_copy(slot, src, k).start()

    forward_x(me, block_ref)
    counts = (n // 2, n - 1 - n // 2)
    targets = (right, left)
    signs = (-1, 1)
    sent = ([], [])
    for step in range(max(counts)):
        for d in range(2):
            if step >= counts[d]:
                continue
            slot = lax.rem(me + signs[d] * step + n, n)
            if step > 0:
                sent[d][step - 1].wait_recv()
                forward_x(slot, ring_ref.at[slot])
            src = block_ref if step == 0 else ring_ref.at[slot]
            copy = pltpu.make_async_remote_copy(
                src_ref=src,
                dst_ref=ring_ref.at[slot],
                send_sem=send_sem.at[d, step],
                recv_sem=recv_sem.at[d, step],
                device_id=on_ring(targets[d]),
                device_id_type=MESH_IDS,
            )
            copy.start()
            sent[d].append(copy)
    for d in range(2):
        if sent[d]:
            sent[d][-1].wait_recv()
            last = lax.rem(me + signs[d] * counts[d] + n, n)
            forward_x(last, ring_ref.at[last])
        for copy in sent[d]:
            copy.wait_send()

    @pl.when(is_source)
    def _():
        for slot in range(n):
            for k in range(1, n_x):
                x_copy(slot, ring_ref.at[slot], k).wait_send()
        local = pltpu.make_async_copy(ring_ref, moved_ref, local_sem.at[0])
        local.start()
        local.wait()

    @pl.when(jnp.logical_not(is_source))
    def _():
        whole = pltpu.make_async_remote_copy(
            src_ref=ring_ref,
            dst_ref=moved_ref,
            send_sem=local_sem.at[0],
            recv_sem=xrecv_sem.at[0],
            device_id={"x": col},
            device_id_type=MESH_IDS,
        )
        whole.wait_recv()


def front_exchange(block, n_x, n_zh, n_c):
    n = n_zh * n_c
    steps = max(n // 2, 1)
    shape = jax.ShapeDtypeStruct((n,) + block.shape, block.dtype)
    return pl.pallas_call(
        functools.partial(_front_kernel, n_x, n_zh, n_c),
        out_shape=(shape, shape),
        in_specs=[pl.BlockSpec(memory_space=pltpu.VMEM)],
        out_specs=(pl.BlockSpec(memory_space=pltpu.VMEM), pl.BlockSpec(memory_space=pltpu.VMEM)),
        scratch_shapes=[
            pltpu.SemaphoreType.DMA((2, steps)),
            pltpu.SemaphoreType.DMA((2, steps)),
            pltpu.SemaphoreType.DMA((n, max(n_x - 1, 1))),
            pltpu.SemaphoreType.DMA((1,)),
            pltpu.SemaphoreType.DMA((1,)),
        ],
        compiler_params=pltpu.CompilerParams(collective_id=0, has_side_effects=True),
    )(block)

def _add_tiles_kernel(tile_cols, tiles_dev, ids_ref, base_ref, vals_ref, out_ref):
    out_ref[...] = base_ref[...]
    tile_rows, tile_width = vals_ref.shape[1], vals_ref.shape[2]

    def body(i, carry):
        tile = ids_ref[i]

        @pl.when(tile < tiles_dev)
        def _():
            rows = pl.ds(pl.multiple_of((tile // tile_cols) * tile_rows, tile_rows), tile_rows)
            cols = pl.ds(pl.multiple_of((tile % tile_cols) * tile_width, tile_width), tile_width)
            out_ref[rows, cols] = out_ref[rows, cols] + vals_ref[i]

        return carry

    lax.fori_loop(0, vals_ref.shape[0], body, 0)


def add_tiles(ids, base, vals, tile_cols, tiles_dev):
    vmem = pl.BlockSpec(memory_space=pltpu.VMEM)
    return pl.pallas_call(
        functools.partial(_add_tiles_kernel, tile_cols, tiles_dev),
        out_shape=jax.ShapeDtypeStruct(base.shape, base.dtype),
        in_specs=[pl.BlockSpec(memory_space=pltpu.SMEM), vmem, vmem],
        out_specs=vmem,
    )(ids, base, vals)

def per_device(diag_inverse, panel, trailing, agg_vals, agg_dest, agg_tile):
    row_devices = lax.axis_size(ROW_AXES)
    local_rows, local_cols = trailing.shape
    panel_width = diag_inverse.shape[0]
    part_width = panel.shape[1]
    col_index = lax.axis_index("col")
    zh_index = lax.axis_index("zh")

    tile_rows = local_rows // TILE_ROWS
    tile_cols = local_cols // TILE_COLS
    tiles_dev = tile_rows * tile_cols
    tile_values = agg_vals.reshape(agg_vals.shape[2], agg_vals.shape[3])
    targets = agg_dest.reshape(-1)
    tile_ids = agg_tile.reshape(-1)
    matches = (targets[:, None] == jnp.arange(row_devices, dtype=jnp.int32)[None, :]).astype(
        jnp.int32
    )
    earlier = jnp.cumsum(matches, axis=0) - matches
    ranks = jnp.sum(earlier * matches, axis=1)
    position = targets * CAP + ranks
    id_lanes = jnp.broadcast_to(tile_ids.astype(jnp.float32)[:, None], (tile_ids.shape[0], TILE_COLS))
    payload = jnp.concatenate([tile_values, id_lanes], axis=1)
    send = (
        jnp.zeros((row_devices * CAP, payload.shape[1]), jnp.float32)
        .at[:, tile_values.shape[1]:]
        .set(float(tiles_dev))
        .at[position]
        .set(payload)
    )
    got = lax.all_to_all(send, ROW_AXES, split_axis=0, concat_axis=0, tiled=True)
    got_values = got[:, : tile_values.shape[1]]
    landing = got[:, tile_values.shape[1]].astype(jnp.int32)

    n_zh = lax.axis_size("zh")
    n_c = lax.axis_size("col")
    n_x = lax.axis_size("x")
    ring_panel, moved_panel = front_exchange(panel, n_x, n_zh, n_c)

    def to_rows(blocks):
        blocks = blocks.reshape(n_zh, n_c, local_rows, part_width).transpose(0, 2, 1, 3)
        return blocks.reshape(n_zh * local_rows, n_c * part_width)

    own_panel = lax.dynamic_index_in_dim(
        to_rows(ring_panel).reshape(n_zh, local_rows, panel_width), zh_index, 0, keepdims=False
    )
    own_full = jnp.dot(
        own_panel,
        diag_inverse.T,
        precision=lax.Precision.HIGHEST,
        preferred_element_type=jnp.float32,
    )
    own_block = lax.dynamic_slice_in_dim(own_full, col_index * part_width, part_width, 1)
    chosen = jnp.dot(
        to_rows(moved_panel),
        diag_inverse.T,
        precision=lax.Precision.HIGHEST,
        preferred_element_type=jnp.float32,
    ).reshape(n_zh, local_rows, panel_width)
    gathered = lax.all_gather(chosen, ("y", "core"), axis=1, tiled=False)
    partner = gathered.reshape(local_cols, panel_width)

    product = lax.dot_general(
        own_full,
        partner,
        (((1,), (1,)), ((), ())),
        precision=lax.Precision.HIGH,
        preferred_element_type=jnp.float32,
    )
    updated = add_tiles(
        landing,
        trailing - product,
        got_values.reshape(-1, TILE_ROWS, TILE_COLS),
        tile_cols,
        tiles_dev,
    )
    return (updated, own_block)


def solution(mesh):
    n_row, n_col = mesh.devices.shape
    shape = (n_col, n_col, n_col, n_row // n_col**3, n_col)
    split = Mesh(mesh.devices.reshape(shape), ROW_AXES + ("col",))
    rows = ROW_AXES
    in_specs = (
        P(),
        P(rows, "col"),
        P(rows, "col"),
        P(rows, "col", None, None),
        P(rows, "col", None, None),
        P(rows, "col", None),
    )
    out_specs = (P(rows, "col"), P(rows, "col"))
    return jax.shard_map(
        per_device, mesh=split, in_specs=in_specs, out_specs=out_specs, check_vma=False
    )
```

```python
import functools

import jax
import jax.numpy as jnp
from jax import lax
from jax.experimental import pallas as pl
from jax.experimental.pallas import tpu as pltpu
from jax.sharding import Mesh
from jax.sharding import PartitionSpec as P

TILE_ROWS = 8
TILE_COLS = 128
CAP = 2
ROW_AXES = ("x", "zh", "y", "core")
MESH_IDS = pl.DeviceIdType.MESH


def _front_kernel(n_x, n_zh, n_c, block_ref, ring_ref, moved_ref, send_sem, recv_sem,
                  xsend_sem, xrecv_sem, xfwd_sem, local_sem):
    n = n_zh * n_c
    col = lax.axis_index("col")
    x = lax.axis_index("x")
    me = lax.axis_index("zh") * n_c + col
    right = lax.rem(me + 1, n)
    left = lax.rem(me + n - 1, n)
    shift = lax.rem(x - col + n_x, n_x)
    x_up = lax.rem(x + 1, n_x)
    x_down = lax.rem(x + n_x - 1, n_x)

    def on_ring(p):
        return {"zh": p // n_c, "col": lax.rem(p, n_c)}

    barrier = pltpu.get_barrier_semaphore()
    for other in (left, right):
        pl.semaphore_signal(barrier, 1, device_id=on_ring(other), device_id_type=MESH_IDS)
    for other in (x_up, x_down):
        pl.semaphore_signal(barrier, 1, device_id={"x": other}, device_id_type=MESH_IDS)
    pl.semaphore_wait(barrier, 4)

    ring_ref[me] = block_ref[...]

    def x_copy(slot, src, target, send):
        return pltpu.make_async_remote_copy(
            src_ref=src,
            dst_ref=moved_ref.at[slot],
            send_sem=send,
            recv_sem=xrecv_sem.at[slot],
            device_id={"x": target},
            device_id_type=MESH_IDS,
        )

    order = []

    def x_stage(slot, src):
        t = len(order)
        order.append(slot)

        @pl.when(shift == 0)
        def _():
            x_copy(slot, src, x_up, xsend_sem.at[slot, 0]).start()
            x_copy(slot, src, x_down, xsend_sem.at[slot, 1]).start()

        for role, parity, onward in ((1, 0, x_up), (n_x - 1, 1, x_down)):
            @pl.when(shift == role)
            def _():
                x_copy(slot, moved_ref.at[slot], onward, xfwd_sem.at[slot]).wait_recv()
                if t % 2 == parity:
                    x_copy(slot, moved_ref.at[slot], onward, xfwd_sem.at[slot]).start()

    x_stage(me, block_ref)
    counts = (n // 2, n - 1 - n // 2)
    targets = (right, left)
    signs = (-1, 1)
    sent = ([], [])
    for step in range(max(counts)):
        for d in range(2):
            if step >= counts[d]:
                continue
            slot = lax.rem(me + signs[d] * step + n, n)
            if step > 0:
                sent[d][step - 1].wait_recv()
                x_stage(slot, ring_ref.at[slot])
            src = block_ref if step == 0 else ring_ref.at[slot]
            copy = pltpu.make_async_remote_copy(
                src_ref=src,
                dst_ref=ring_ref.at[slot],
                send_sem=send_sem.at[d, step],
                recv_sem=recv_sem.at[d, step],
                device_id=on_ring(targets[d]),
                device_id_type=MESH_IDS,
            )
            copy.start()
            sent[d].append(copy)
    for d in range(2):
        if sent[d]:
            sent[d][-1].wait_recv()
            last = lax.rem(me + signs[d] * counts[d] + n, n)
            x_stage(last, ring_ref.at[last])
        for copy in sent[d]:
            copy.wait_send()

    @pl.when(shift == 0)
    def _():
        for slot in order:
            x_copy(slot, ring_ref.at[slot], x_up, xsend_sem.at[slot, 0]).wait_send()
            x_copy(slot, ring_ref.at[slot], x_down, xsend_sem.at[slot, 1]).wait_send()
        local = pltpu.make_async_copy(ring_ref, moved_ref, local_sem.at[0])
        local.start()
        local.wait()

    for role, parity, onward in ((1, 0, x_up), (n_x - 1, 1, x_down)):
        @pl.when(shift == role)
        def _():
            for t, slot in enumerate(order):
                if t % 2 == parity:
                    x_copy(slot, moved_ref.at[slot], onward, xfwd_sem.at[slot]).wait_send()

    @pl.when(shift == 2)
    def _():
        for slot in order:
            x_copy(slot, moved_ref.at[slot], x_up, xfwd_sem.at[slot]).wait_recv()


def front_exchange(block, n_x, n_zh, n_c):
    n = n_zh * n_c
    steps = max(n // 2, 1)
    shape = jax.ShapeDtypeStruct((n,) + block.shape, block.dtype)
    return pl.pallas_call(
        functools.partial(_front_kernel, n_x, n_zh, n_c),
        out_shape=(shape, shape),
        in_specs=[pl.BlockSpec(memory_space=pltpu.VMEM)],
        out_specs=(pl.BlockSpec(memory_space=pltpu.VMEM), pl.BlockSpec(memory_space=pltpu.VMEM)),
        scratch_shapes=[
            pltpu.SemaphoreType.DMA((2, steps)),
            pltpu.SemaphoreType.DMA((2, steps)),
            pltpu.SemaphoreType.DMA((n, 2)),
            pltpu.SemaphoreType.DMA((n,)),
            pltpu.SemaphoreType.DMA((n,)),
            pltpu.SemaphoreType.DMA((1,)),
        ],
        compiler_params=pltpu.CompilerParams(collective_id=0, has_side_effects=True),
    )(block)

def _add_tiles_kernel(tile_cols, tiles_dev, ids_ref, base_ref, vals_ref, out_ref):
    out_ref[...] = base_ref[...]
    tile_rows, tile_width = vals_ref.shape[1], vals_ref.shape[2]

    def body(i, carry):
        tile = ids_ref[i]

        @pl.when(tile < tiles_dev)
        def _():
            rows = pl.ds(pl.multiple_of((tile // tile_cols) * tile_rows, tile_rows), tile_rows)
            cols = pl.ds(pl.multiple_of((tile % tile_cols) * tile_width, tile_width), tile_width)
            out_ref[rows, cols] = out_ref[rows, cols] + vals_ref[i]

        return carry

    lax.fori_loop(0, vals_ref.shape[0], body, 0)


def add_tiles(ids, base, vals, tile_cols, tiles_dev):
    vmem = pl.BlockSpec(memory_space=pltpu.VMEM)
    return pl.pallas_call(
        functools.partial(_add_tiles_kernel, tile_cols, tiles_dev),
        out_shape=jax.ShapeDtypeStruct(base.shape, base.dtype),
        in_specs=[pl.BlockSpec(memory_space=pltpu.SMEM), vmem, vmem],
        out_specs=vmem,
    )(ids, base, vals)

def per_device(diag_inverse, panel, trailing, agg_vals, agg_dest, agg_tile):
    row_devices = lax.axis_size(ROW_AXES)
    local_rows, local_cols = trailing.shape
    panel_width = diag_inverse.shape[0]
    part_width = panel.shape[1]
    col_index = lax.axis_index("col")
    zh_index = lax.axis_index("zh")

    tile_rows = local_rows // TILE_ROWS
    tile_cols = local_cols // TILE_COLS
    tiles_dev = tile_rows * tile_cols
    tile_values = agg_vals.reshape(agg_vals.shape[2], agg_vals.shape[3])
    targets = agg_dest.reshape(-1)
    tile_ids = agg_tile.reshape(-1)
    matches = (targets[:, None] == jnp.arange(row_devices, dtype=jnp.int32)[None, :]).astype(
        jnp.int32
    )
    earlier = jnp.cumsum(matches, axis=0) - matches
    ranks = jnp.sum(earlier * matches, axis=1)
    position = targets * CAP + ranks
    id_lanes = jnp.broadcast_to(tile_ids.astype(jnp.float32)[:, None], (tile_ids.shape[0], TILE_COLS))
    payload = jnp.concatenate([tile_values, id_lanes], axis=1)
    send = (
        jnp.zeros((row_devices * CAP, payload.shape[1]), jnp.float32)
        .at[:, tile_values.shape[1]:]
        .set(float(tiles_dev))
        .at[position]
        .set(payload)
    )
    got = lax.all_to_all(send, ROW_AXES, split_axis=0, concat_axis=0, tiled=True)
    got_values = got[:, : tile_values.shape[1]]
    landing = got[:, tile_values.shape[1]].astype(jnp.int32)

    n_zh = lax.axis_size("zh")
    n_c = lax.axis_size("col")
    n_x = lax.axis_size("x")
    ring_panel, moved_panel = front_exchange(panel, n_x, n_zh, n_c)

    def to_rows(blocks):
        blocks = blocks.reshape(n_zh, n_c, local_rows, part_width).transpose(0, 2, 1, 3)
        return blocks.reshape(n_zh * local_rows, n_c * part_width)

    own_panel = lax.dynamic_index_in_dim(
        to_rows(ring_panel).reshape(n_zh, local_rows, panel_width), zh_index, 0, keepdims=False
    )
    own_full = jnp.dot(
        own_panel,
        diag_inverse.T,
        precision=lax.Precision.HIGHEST,
        preferred_element_type=jnp.float32,
    )
    own_block = lax.dynamic_slice_in_dim(own_full, col_index * part_width, part_width, 1)
    chosen = jnp.dot(
        to_rows(moved_panel),
        diag_inverse.T,
        precision=lax.Precision.HIGHEST,
        preferred_element_type=jnp.float32,
    ).reshape(n_zh, local_rows, panel_width)
    gathered = lax.all_gather(chosen, ("y", "core"), axis=1, tiled=False)
    partner = gathered.reshape(local_cols, panel_width)

    product = lax.dot_general(
        own_full,
        partner,
        (((1,), (1,)), ((), ())),
        precision=lax.Precision.HIGH,
        preferred_element_type=jnp.float32,
    )
    updated = add_tiles(
        landing,
        trailing - product,
        got_values.reshape(-1, TILE_ROWS, TILE_COLS),
        tile_cols,
        tiles_dev,
    )
    return (updated, own_block)


def solution(mesh):
    n_row, n_col = mesh.devices.shape
    shape = (n_col, n_col, n_col, n_row // n_col**3, n_col)
    split = Mesh(mesh.devices.reshape(shape), ROW_AXES + ("col",))
    rows = ROW_AXES
    in_specs = (
        P(),
        P(rows, "col"),
        P(rows, "col"),
        P(rows, "col", None, None),
        P(rows, "col", None, None),
        P(rows, "col", None),
    )
    out_specs = (P(rows, "col"), P(rows, "col"))
    return jax.shard_map(
        per_device, mesh=split, in_specs=in_specs, out_specs=out_specs, check_vma=False
    )
```

```python
import functools

import jax
import jax.numpy as jnp
from jax import lax
from jax.experimental import pallas as pl
from jax.experimental.pallas import tpu as pltpu
from jax.sharding import Mesh
from jax.sharding import PartitionSpec as P

TILE_ROWS = 8
TILE_COLS = 128
CAP = 2
ROW_AXES = ("x", "zh", "y", "core")
MESH_IDS = pl.DeviceIdType.MESH


def _front_kernel(n_x, n_zh, n_c, block_ref, ring_ref, moved_ref, send_sem, recv_sem,
                  xsend_sem, xrecv_sem, local_sem):
    n = n_zh * n_c
    col = lax.axis_index("col")
    x = lax.axis_index("x")
    me = lax.axis_index("zh") * n_c + col
    right = lax.rem(me + 1, n)
    left = lax.rem(me + n - 1, n)
    is_source = x == col

    def on_ring(p):
        return {"zh": p // n_c, "col": lax.rem(p, n_c)}

    def x_peer(k):
        return {"x": lax.rem(x + k, n_x)}

    barrier = pltpu.get_barrier_semaphore()
    for other in (left, right):
        pl.semaphore_signal(barrier, 1, device_id=on_ring(other), device_id_type=MESH_IDS)

    @pl.when(is_source)
    def _():
        for k in range(1, n_x):
            pl.semaphore_signal(barrier, 1, device_id=x_peer(k), device_id_type=MESH_IDS)
        pl.semaphore_wait(barrier, 2 + n_x - 1)

    @pl.when(jnp.logical_not(is_source))
    def _():
        pl.semaphore_signal(barrier, 1, device_id={"x": col}, device_id_type=MESH_IDS)
        pl.semaphore_wait(barrier, 3)

    ring_ref[me] = block_ref[...]

    def x_copy(slot, src, k):
        return pltpu.make_async_remote_copy(
            src_ref=src,
            dst_ref=moved_ref.at[slot],
            send_sem=xsend_sem.at[slot, k - 1],
            recv_sem=xrecv_sem.at[0],
            device_id=x_peer(k),
            device_id_type=MESH_IDS,
        )

    def forward_x(slot, src):
        @pl.when(is_source)
        def _():
            for k in range(1, n_x):
                x_copy(slot, src, k).start()

    counts = (n // 2, n - 1 - n // 2)
    targets = (right, left)
    signs = (-1, 1)
    sent = ([], [])
    for step in range(max(counts) + 1):
        ready = []
        for d in range(2):
            if step > counts[d]:
                continue
            slot = lax.rem(me + signs[d] * step + n, n)
            if step > 0:
                sent[d][step - 1].wait_recv()
                ready.append(slot)
            if step < counts[d]:
                src = block_ref if step == 0 else ring_ref.at[slot]
                copy = pltpu.make_async_remote_copy(
                    src_ref=src,
                    dst_ref=ring_ref.at[slot],
                    send_sem=send_sem.at[d, step],
                    recv_sem=recv_sem.at[d, step],
                    device_id=on_ring(targets[d]),
                    device_id_type=MESH_IDS,
                )
                copy.start()
                sent[d].append(copy)
        if step == 0:
            forward_x(me, block_ref)
        for slot in ready:
            forward_x(slot, ring_ref.at[slot])
    for d in range(2):
        for copy in sent[d]:
            copy.wait_send()

    @pl.when(is_source)
    def _():
        for slot in range(n):
            for k in range(1, n_x):
                x_copy(slot, ring_ref.at[slot], k).wait_send()
        local = pltpu.make_async_copy(ring_ref, moved_ref, local_sem.at[0])
        local.start()
        local.wait()

    @pl.when(jnp.logical_not(is_source))
    def _():
        whole = pltpu.make_async_remote_copy(
            src_ref=ring_ref,
            dst_ref=moved_ref,
            send_sem=local_sem.at[0],
            recv_sem=xrecv_sem.at[0],
            device_id={"x": col},
            device_id_type=MESH_IDS,
        )
        whole.wait_recv()


def front_exchange(block, n_x, n_zh, n_c):
    n = n_zh * n_c
    steps = max(n // 2, 1)
    shape = jax.ShapeDtypeStruct((n,) + block.shape, block.dtype)
    return pl.pallas_call(
        functools.partial(_front_kernel, n_x, n_zh, n_c),
        out_shape=(shape, shape),
        in_specs=[pl.BlockSpec(memory_space=pltpu.VMEM)],
        out_specs=(pl.BlockSpec(memory_space=pltpu.VMEM), pl.BlockSpec(memory_space=pltpu.VMEM)),
        scratch_shapes=[
            pltpu.SemaphoreType.DMA((2, steps)),
            pltpu.SemaphoreType.DMA((2, steps)),
            pltpu.SemaphoreType.DMA((n, max(n_x - 1, 1))),
            pltpu.SemaphoreType.DMA((1,)),
            pltpu.SemaphoreType.DMA((1,)),
        ],
        compiler_params=pltpu.CompilerParams(collective_id=0, has_side_effects=True),
    )(block)

def _add_tiles_kernel(tile_cols, tiles_dev, ids_ref, base_ref, vals_ref, out_ref):
    out_ref[...] = base_ref[...]
    tile_rows, tile_width = vals_ref.shape[1], vals_ref.shape[2]

    def body(i, carry):
        tile = ids_ref[i]

        @pl.when(tile < tiles_dev)
        def _():
            rows = pl.ds(pl.multiple_of((tile // tile_cols) * tile_rows, tile_rows), tile_rows)
            cols = pl.ds(pl.multiple_of((tile % tile_cols) * tile_width, tile_width), tile_width)
            out_ref[rows, cols] = out_ref[rows, cols] + vals_ref[i]

        return carry

    lax.fori_loop(0, vals_ref.shape[0], body, 0)


def add_tiles(ids, base, vals, tile_cols, tiles_dev):
    vmem = pl.BlockSpec(memory_space=pltpu.VMEM)
    return pl.pallas_call(
        functools.partial(_add_tiles_kernel, tile_cols, tiles_dev),
        out_shape=jax.ShapeDtypeStruct(base.shape, base.dtype),
        in_specs=[pl.BlockSpec(memory_space=pltpu.SMEM), vmem, vmem],
        out_specs=vmem,
    )(ids, base, vals)

def per_device(diag_inverse, panel, trailing, agg_vals, agg_dest, agg_tile):
    row_devices = lax.axis_size(ROW_AXES)
    local_rows, local_cols = trailing.shape
    panel_width = diag_inverse.shape[0]
    part_width = panel.shape[1]
    col_index = lax.axis_index("col")
    zh_index = lax.axis_index("zh")

    tile_rows = local_rows // TILE_ROWS
    tile_cols = local_cols // TILE_COLS
    tiles_dev = tile_rows * tile_cols
    tile_values = agg_vals.reshape(agg_vals.shape[2], agg_vals.shape[3])
    targets = agg_dest.reshape(-1)
    tile_ids = agg_tile.reshape(-1)
    matches = (targets[:, None] == jnp.arange(row_devices, dtype=jnp.int32)[None, :]).astype(
        jnp.int32
    )
    earlier = jnp.cumsum(matches, axis=0) - matches
    ranks = jnp.sum(earlier * matches, axis=1)
    position = targets * CAP + ranks
    id_lanes = jnp.broadcast_to(tile_ids.astype(jnp.float32)[:, None], (tile_ids.shape[0], TILE_COLS))
    payload = jnp.concatenate([tile_values, id_lanes], axis=1)
    send = (
        jnp.zeros((row_devices * CAP, payload.shape[1]), jnp.float32)
        .at[:, tile_values.shape[1]:]
        .set(float(tiles_dev))
        .at[position]
        .set(payload)
    )
    got = lax.all_to_all(send, ROW_AXES, split_axis=0, concat_axis=0, tiled=True)
    got_values = got[:, : tile_values.shape[1]]
    landing = got[:, tile_values.shape[1]].astype(jnp.int32)

    n_zh = lax.axis_size("zh")
    n_c = lax.axis_size("col")
    n_x = lax.axis_size("x")
    ring_panel, moved_panel = front_exchange(panel, n_x, n_zh, n_c)

    def to_rows(blocks):
        blocks = blocks.reshape(n_zh, n_c, local_rows, part_width).transpose(0, 2, 1, 3)
        return blocks.reshape(n_zh * local_rows, n_c * part_width)

    own_panel = lax.dynamic_index_in_dim(
        to_rows(ring_panel).reshape(n_zh, local_rows, panel_width), zh_index, 0, keepdims=False
    )
    own_full = jnp.dot(
        own_panel,
        diag_inverse.T,
        precision=lax.Precision.HIGHEST,
        preferred_element_type=jnp.float32,
    )
    own_block = lax.dynamic_slice_in_dim(own_full, col_index * part_width, part_width, 1)
    chosen = jnp.dot(
        to_rows(moved_panel),
        diag_inverse.T,
        precision=lax.Precision.HIGHEST,
        preferred_element_type=jnp.float32,
    ).reshape(n_zh, local_rows, panel_width)
    gathered = lax.all_gather(chosen, ("y", "core"), axis=1, tiled=False)
    partner = gathered.reshape(local_cols, panel_width)

    product = lax.dot_general(
        own_full,
        partner,
        (((1,), (1,)), ((), ())),
        precision=lax.Precision.HIGH,
        preferred_element_type=jnp.float32,
    )
    updated = add_tiles(
        landing,
        trailing - product,
        got_values.reshape(-1, TILE_ROWS, TILE_COLS),
        tile_cols,
        tiles_dev,
    )
    return (updated, own_block)


def solution(mesh):
    n_row, n_col = mesh.devices.shape
    shape = (n_col, n_col, n_col, n_row // n_col**3, n_col)
    split = Mesh(mesh.devices.reshape(shape), ROW_AXES + ("col",))
    rows = ROW_AXES
    in_specs = (
        P(),
        P(rows, "col"),
        P(rows, "col"),
        P(rows, "col", None, None),
        P(rows, "col", None, None),
        P(rows, "col", None),
    )
    out_specs = (P(rows, "col"), P(rows, "col"))
    return jax.shard_map(
        per_device, mesh=split, in_specs=in_specs, out_specs=out_specs, check_vma=False
    )
```

```python
import functools

import jax
import jax.numpy as jnp
from jax import lax
from jax.experimental import pallas as pl
from jax.experimental.pallas import tpu as pltpu
from jax.sharding import Mesh
from jax.sharding import PartitionSpec as P

TILE_ROWS = 8
TILE_COLS = 128
CAP = 2
ROW_AXES = ("x", "zh", "y", "core")
MESH_IDS = pl.DeviceIdType.MESH


def _front_kernel(n_x, n_zh, n_c, block_ref, ring_ref, moved_ref, send_sem, recv_sem,
                  xsend_sem, xrecv_sem, local_sem):
    n = n_zh * n_c
    col = lax.axis_index("col")
    x = lax.axis_index("x")
    me = lax.axis_index("zh") * n_c + col
    right = lax.rem(me + 1, n)
    left = lax.rem(me + n - 1, n)
    is_source = x == col

    def on_ring(p):
        return {"zh": p // n_c, "col": lax.rem(p, n_c)}

    def x_peer(k):
        return {"x": lax.rem(x + k, n_x)}

    barrier = pltpu.get_barrier_semaphore()
    for other in (left, right):
        pl.semaphore_signal(barrier, 1, device_id=on_ring(other), device_id_type=MESH_IDS)

    @pl.when(is_source)
    def _():
        for k in range(1, n_x):
            pl.semaphore_signal(barrier, 1, device_id=x_peer(k), device_id_type=MESH_IDS)
        pl.semaphore_wait(barrier, 2 + n_x - 1)

    @pl.when(jnp.logical_not(is_source))
    def _():
        pl.semaphore_signal(barrier, 1, device_id={"x": col}, device_id_type=MESH_IDS)
        pl.semaphore_wait(barrier, 3)

    ring_ref[me] = block_ref[...]

    def x_copy(slot, src, k):
        return pltpu.make_async_remote_copy(
            src_ref=src,
            dst_ref=moved_ref.at[slot],
            send_sem=xsend_sem.at[slot, k - 1],
            recv_sem=xrecv_sem.at[0],
            device_id=x_peer(k),
            device_id_type=MESH_IDS,
        )

    def forward_x(slot, src):
        @pl.when(is_source)
        def _():
            for k in range(1, n_x):
                x_copy(slot, src, k).start()

    counts = (n // 2, n - 1 - n // 2)
    targets = (right, left)
    signs = (-1, 1)
    sent = ([], [])
    for step in range(max(counts) + 1):
        ready = []
        for d in range(2):
            if step > counts[d]:
                continue
            slot = lax.rem(me + signs[d] * step + n, n)
            if step > 0:
                sent[d][step - 1].wait_recv()
                ready.append(slot)
            if step < counts[d]:
                src = block_ref if step == 0 else ring_ref.at[slot]
                copy = pltpu.make_async_remote_copy(
                    src_ref=src,
                    dst_ref=ring_ref.at[slot],
                    send_sem=send_sem.at[d, step],
                    recv_sem=recv_sem.at[d, step],
                    device_id=on_ring(targets[d]),
                    device_id_type=MESH_IDS,
                )
                copy.start()
                sent[d].append(copy)
        if step == 0:
            forward_x(me, block_ref)
        for slot in ready:
            forward_x(slot, ring_ref.at[slot])
    for d in range(2):
        for copy in sent[d]:
            copy.wait_send()

    @pl.when(is_source)
    def _():
        for slot in range(n):
            for k in range(1, n_x):
                x_copy(slot, ring_ref.at[slot], k).wait_send()
        local = pltpu.make_async_copy(ring_ref, moved_ref, local_sem.at[0])
        local.start()
        local.wait()

    @pl.when(jnp.logical_not(is_source))
    def _():
        whole = pltpu.make_async_remote_copy(
            src_ref=ring_ref,
            dst_ref=moved_ref,
            send_sem=local_sem.at[0],
            recv_sem=xrecv_sem.at[0],
            device_id={"x": col},
            device_id_type=MESH_IDS,
        )
        whole.wait_recv()


def front_exchange(block, n_x, n_zh, n_c):
    n = n_zh * n_c
    steps = max(n // 2, 1)
    shape = jax.ShapeDtypeStruct((n,) + block.shape, block.dtype)
    return pl.pallas_call(
        functools.partial(_front_kernel, n_x, n_zh, n_c),
        out_shape=(shape, shape),
        in_specs=[pl.BlockSpec(memory_space=pltpu.VMEM)],
        out_specs=(pl.BlockSpec(memory_space=pltpu.VMEM), pl.BlockSpec(memory_space=pltpu.VMEM)),
        scratch_shapes=[
            pltpu.SemaphoreType.DMA((2, steps)),
            pltpu.SemaphoreType.DMA((2, steps)),
            pltpu.SemaphoreType.DMA((n, max(n_x - 1, 1))),
            pltpu.SemaphoreType.DMA((1,)),
            pltpu.SemaphoreType.DMA((1,)),
        ],
        compiler_params=pltpu.CompilerParams(collective_id=0, has_side_effects=True),
    )(block)

def _add_tiles_kernel(tile_cols, tiles_dev, ids_ref, base_ref, vals_ref, out_ref):
    out_ref[...] = base_ref[...]
    tile_rows, tile_width = vals_ref.shape[1], vals_ref.shape[2]

    def body(i, carry):
        tile = ids_ref[i]

        @pl.when(tile < tiles_dev)
        def _():
            rows = pl.ds(pl.multiple_of((tile // tile_cols) * tile_rows, tile_rows), tile_rows)
            cols = pl.ds(pl.multiple_of((tile % tile_cols) * tile_width, tile_width), tile_width)
            out_ref[rows, cols] = out_ref[rows, cols] + vals_ref[i]

        return carry

    lax.fori_loop(0, vals_ref.shape[0], body, 0)


def add_tiles(ids, base, vals, tile_cols, tiles_dev):
    vmem = pl.BlockSpec(memory_space=pltpu.VMEM)
    return pl.pallas_call(
        functools.partial(_add_tiles_kernel, tile_cols, tiles_dev),
        out_shape=jax.ShapeDtypeStruct(base.shape, base.dtype),
        in_specs=[pl.BlockSpec(memory_space=pltpu.SMEM), vmem, vmem],
        out_specs=vmem,
    )(ids, base, vals)

def _spread_kernel(n_y, n_core, block_ref, out_ref, send_sem, recv_sem, local_sem):
    n = n_y * n_core
    me = lax.axis_index("y") * n_core + lax.axis_index("core")

    def where(p):
        return {"y": p // n_core, "core": lax.rem(p, n_core)}

    barrier = pltpu.get_barrier_semaphore()
    for k in range(1, n):
        pl.semaphore_signal(barrier, 1, device_id=where(lax.rem(me + k, n)), device_id_type=MESH_IDS)
    pl.semaphore_wait(barrier, n - 1)
    parts = block_ref.shape[0]
    local = []
    for j in range(parts):
        copy = pltpu.make_async_copy(block_ref.at[j], out_ref.at[j, me], local_sem.at[j])
        copy.start()
        local.append(copy)
    for k in range(1, n):
        peer = where(lax.rem(me + k, n))
        for j in range(parts):
            pltpu.make_async_remote_copy(
                src_ref=block_ref.at[j],
                dst_ref=out_ref.at[j, me],
                send_sem=send_sem.at[0],
                recv_sem=recv_sem.at[0],
                device_id=peer,
                device_id_type=MESH_IDS,
            ).start()
    every = pltpu.make_async_remote_copy(
        src_ref=out_ref.at[:, pl.ds(0, n - 1)],
        dst_ref=out_ref.at[:, pl.ds(0, n - 1)],
        send_sem=send_sem.at[0],
        recv_sem=recv_sem.at[0],
        device_id=where(lax.rem(me + 1, n)),
        device_id_type=MESH_IDS,
    )
    every.wait_send()
    every.wait_recv()
    for copy in local:
        copy.wait()


def spread(block, n_y, n_core):
    n = n_y * n_core
    parts = block.shape[0]
    anywhere = pl.BlockSpec(memory_space=pl.ANY)
    return pl.pallas_call(
        functools.partial(_spread_kernel, n_y, n_core),
        out_shape=jax.ShapeDtypeStruct((parts, n) + block.shape[1:], block.dtype),
        in_specs=[anywhere],
        out_specs=anywhere,
        scratch_shapes=[
            pltpu.SemaphoreType.DMA((1,)),
            pltpu.SemaphoreType.DMA((1,)),
            pltpu.SemaphoreType.DMA((parts,)),
        ],
        compiler_params=pltpu.CompilerParams(collective_id=1, has_side_effects=True),
    )(block)

def per_device(diag_inverse, panel, trailing, agg_vals, agg_dest, agg_tile):
    row_devices = lax.axis_size(ROW_AXES)
    local_rows, local_cols = trailing.shape
    panel_width = diag_inverse.shape[0]
    part_width = panel.shape[1]
    col_index = lax.axis_index("col")
    zh_index = lax.axis_index("zh")

    tile_rows = local_rows // TILE_ROWS
    tile_cols = local_cols // TILE_COLS
    tiles_dev = tile_rows * tile_cols
    tile_values = agg_vals.reshape(agg_vals.shape[2], agg_vals.shape[3])
    targets = agg_dest.reshape(-1)
    tile_ids = agg_tile.reshape(-1)
    matches = (targets[:, None] == jnp.arange(row_devices, dtype=jnp.int32)[None, :]).astype(
        jnp.int32
    )
    earlier = jnp.cumsum(matches, axis=0) - matches
    ranks = jnp.sum(earlier * matches, axis=1)
    position = targets * CAP + ranks
    id_lanes = jnp.broadcast_to(tile_ids.astype(jnp.float32)[:, None], (tile_ids.shape[0], TILE_COLS))
    payload = jnp.concatenate([tile_values, id_lanes], axis=1)
    send = (
        jnp.zeros((row_devices * CAP, payload.shape[1]), jnp.float32)
        .at[:, tile_values.shape[1]:]
        .set(float(tiles_dev))
        .at[position]
        .set(payload)
    )
    got = lax.all_to_all(send, ROW_AXES, split_axis=0, concat_axis=0, tiled=True)
    got_values = got[:, : tile_values.shape[1]]
    landing = got[:, tile_values.shape[1]].astype(jnp.int32)

    n_zh = lax.axis_size("zh")
    n_c = lax.axis_size("col")
    n_x = lax.axis_size("x")
    ring_panel, moved_panel = front_exchange(panel, n_x, n_zh, n_c)

    def to_rows(blocks):
        blocks = blocks.reshape(n_zh, n_c, local_rows, part_width).transpose(0, 2, 1, 3)
        return blocks.reshape(n_zh * local_rows, n_c * part_width)

    own_panel = lax.dynamic_index_in_dim(
        to_rows(ring_panel).reshape(n_zh, local_rows, panel_width), zh_index, 0, keepdims=False
    )
    own_full = jnp.dot(
        own_panel,
        diag_inverse.T,
        precision=lax.Precision.HIGHEST,
        preferred_element_type=jnp.float32,
    )
    own_block = lax.dynamic_slice_in_dim(own_full, col_index * part_width, part_width, 1)
    chosen = jnp.dot(
        to_rows(moved_panel),
        diag_inverse.T,
        precision=lax.Precision.HIGHEST,
        preferred_element_type=jnp.float32,
    ).reshape(n_zh, local_rows, panel_width)
    gathered = spread(chosen, lax.axis_size("y"), lax.axis_size("core"))
    partner = gathered.reshape(local_cols, panel_width)

    product = lax.dot_general(
        own_full,
        partner,
        (((1,), (1,)), ((), ())),
        precision=lax.Precision.HIGH,
        preferred_element_type=jnp.float32,
    )
    updated = add_tiles(
        landing,
        trailing - product,
        got_values.reshape(-1, TILE_ROWS, TILE_COLS),
        tile_cols,
        tiles_dev,
    )
    return (updated, own_block)


def solution(mesh):
    n_row, n_col = mesh.devices.shape
    shape = (n_col, n_col, n_col, n_row // n_col**3, n_col)
    split = Mesh(mesh.devices.reshape(shape), ROW_AXES + ("col",))
    rows = ROW_AXES
    in_specs = (
        P(),
        P(rows, "col"),
        P(rows, "col"),
        P(rows, "col", None, None),
        P(rows, "col", None, None),
        P(rows, "col", None),
    )
    out_specs = (P(rows, "col"), P(rows, "col"))
    return jax.shard_map(
        per_device, mesh=split, in_specs=in_specs, out_specs=out_specs, check_vma=False
    )
```

```python
import functools

import jax
import jax.numpy as jnp
from jax import lax
from jax.experimental import pallas as pl
from jax.experimental.pallas import tpu as pltpu
from jax.sharding import Mesh
from jax.sharding import PartitionSpec as P

TILE_ROWS = 8
TILE_COLS = 128
CAP = 2
ROW_AXES = ("x", "zh", "y", "core")
MESH_IDS = pl.DeviceIdType.MESH


def _front_kernel(n_x, n_zh, n_c, block_ref, ring_ref, moved_ref, send_sem, recv_sem,
                  xsend_sem, xrecv_sem, local_sem):
    n = n_zh * n_c
    col = lax.axis_index("col")
    x = lax.axis_index("x")
    me = lax.axis_index("zh") * n_c + col
    right = lax.rem(me + 1, n)
    left = lax.rem(me + n - 1, n)
    is_source = x == col

    def on_ring(p):
        return {"zh": p // n_c, "col": lax.rem(p, n_c)}

    def x_peer(k):
        return {"x": lax.rem(x + k, n_x)}

    barrier = pltpu.get_barrier_semaphore()
    for other in (left, right):
        pl.semaphore_signal(barrier, 1, device_id=on_ring(other), device_id_type=MESH_IDS)

    @pl.when(is_source)
    def _():
        for k in range(1, n_x):
            pl.semaphore_signal(barrier, 1, device_id=x_peer(k), device_id_type=MESH_IDS)
        pl.semaphore_wait(barrier, 2 + n_x - 1)

    @pl.when(jnp.logical_not(is_source))
    def _():
        pl.semaphore_signal(barrier, 1, device_id={"x": col}, device_id_type=MESH_IDS)
        pl.semaphore_wait(barrier, 3)

    ring_ref[me] = block_ref[...]

    def x_copy(slot, src, k):
        return pltpu.make_async_remote_copy(
            src_ref=src,
            dst_ref=moved_ref.at[slot],
            send_sem=xsend_sem.at[slot, k - 1],
            recv_sem=xrecv_sem.at[0],
            device_id=x_peer(k),
            device_id_type=MESH_IDS,
        )

    def forward_x(slot, src):
        @pl.when(is_source)
        def _():
            for k in range(1, n_x):
                x_copy(slot, src, k).start()

    counts = (n // 2, n - 1 - n // 2)
    targets = (right, left)
    signs = (-1, 1)
    sent = ([], [])
    for step in range(max(counts) + 1):
        ready = []
        for d in range(2):
            if step > counts[d]:
                continue
            slot = lax.rem(me + signs[d] * step + n, n)
            if step > 0:
                sent[d][step - 1].wait_recv()
                ready.append(slot)
            if step < counts[d]:
                src = block_ref if step == 0 else ring_ref.at[slot]
                copy = pltpu.make_async_remote_copy(
                    src_ref=src,
                    dst_ref=ring_ref.at[slot],
                    send_sem=send_sem.at[d, step],
                    recv_sem=recv_sem.at[d, step],
                    device_id=on_ring(targets[d]),
                    device_id_type=MESH_IDS,
                )
                copy.start()
                sent[d].append(copy)
        if step == 0:
            forward_x(me, block_ref)
        for slot in ready:
            forward_x(slot, ring_ref.at[slot])
    for d in range(2):
        for copy in sent[d]:
            copy.wait_send()

    @pl.when(is_source)
    def _():
        for slot in range(n):
            for k in range(1, n_x):
                x_copy(slot, ring_ref.at[slot], k).wait_send()
        local = pltpu.make_async_copy(ring_ref, moved_ref, local_sem.at[0])
        local.start()
        local.wait()

    @pl.when(jnp.logical_not(is_source))
    def _():
        whole = pltpu.make_async_remote_copy(
            src_ref=ring_ref,
            dst_ref=moved_ref,
            send_sem=local_sem.at[0],
            recv_sem=xrecv_sem.at[0],
            device_id={"x": col},
            device_id_type=MESH_IDS,
        )
        whole.wait_recv()


def front_exchange(block, n_x, n_zh, n_c):
    n = n_zh * n_c
    steps = max(n // 2, 1)
    shape = jax.ShapeDtypeStruct((n,) + block.shape, block.dtype)
    return pl.pallas_call(
        functools.partial(_front_kernel, n_x, n_zh, n_c),
        out_shape=(shape, shape),
        in_specs=[pl.BlockSpec(memory_space=pltpu.VMEM)],
        out_specs=(pl.BlockSpec(memory_space=pltpu.VMEM), pl.BlockSpec(memory_space=pltpu.VMEM)),
        scratch_shapes=[
            pltpu.SemaphoreType.DMA((2, steps)),
            pltpu.SemaphoreType.DMA((2, steps)),
            pltpu.SemaphoreType.DMA((n, max(n_x - 1, 1))),
            pltpu.SemaphoreType.DMA((1,)),
            pltpu.SemaphoreType.DMA((1,)),
        ],
        compiler_params=pltpu.CompilerParams(collective_id=0, has_side_effects=True),
    )(block)

def _add_tiles_kernel(tile_cols, tiles_dev, ids_ref, base_ref, vals_ref, out_ref):
    out_ref[...] = base_ref[...]
    tile_rows, tile_width = vals_ref.shape[1], vals_ref.shape[2]

    def body(i, carry):
        tile = ids_ref[i]

        @pl.when(tile < tiles_dev)
        def _():
            rows = pl.ds(pl.multiple_of((tile // tile_cols) * tile_rows, tile_rows), tile_rows)
            cols = pl.ds(pl.multiple_of((tile % tile_cols) * tile_width, tile_width), tile_width)
            out_ref[rows, cols] = out_ref[rows, cols] + vals_ref[i]

        return carry

    lax.fori_loop(0, vals_ref.shape[0], body, 0, unroll=8)


def add_tiles(ids, base, vals, tile_cols, tiles_dev):
    vmem = pl.BlockSpec(memory_space=pltpu.VMEM)
    return pl.pallas_call(
        functools.partial(_add_tiles_kernel, tile_cols, tiles_dev),
        out_shape=jax.ShapeDtypeStruct(base.shape, base.dtype),
        in_specs=[pl.BlockSpec(memory_space=pltpu.SMEM), vmem, vmem],
        out_specs=vmem,
    )(ids, base, vals)

def per_device(diag_inverse, panel, trailing, agg_vals, agg_dest, agg_tile):
    row_devices = lax.axis_size(ROW_AXES)
    local_rows, local_cols = trailing.shape
    panel_width = diag_inverse.shape[0]
    part_width = panel.shape[1]
    col_index = lax.axis_index("col")
    zh_index = lax.axis_index("zh")

    tile_rows = local_rows // TILE_ROWS
    tile_cols = local_cols // TILE_COLS
    tiles_dev = tile_rows * tile_cols
    tile_values = agg_vals.reshape(agg_vals.shape[2], agg_vals.shape[3])
    targets = agg_dest.reshape(-1)
    tile_ids = agg_tile.reshape(-1)
    matches = (targets[:, None] == jnp.arange(row_devices, dtype=jnp.int32)[None, :]).astype(
        jnp.int32
    )
    earlier = jnp.cumsum(matches, axis=0) - matches
    ranks = jnp.sum(earlier * matches, axis=1)
    position = targets * CAP + ranks
    id_lanes = jnp.broadcast_to(tile_ids.astype(jnp.float32)[:, None], (tile_ids.shape[0], TILE_COLS))
    payload = jnp.concatenate([tile_values, id_lanes], axis=1)
    send = (
        jnp.zeros((row_devices * CAP, payload.shape[1]), jnp.float32)
        .at[:, tile_values.shape[1]:]
        .set(float(tiles_dev))
        .at[position]
        .set(payload)
    )
    got = lax.all_to_all(send, ROW_AXES, split_axis=0, concat_axis=0, tiled=True)
    got_values = got[:, : tile_values.shape[1]]
    landing = got[:, tile_values.shape[1]].astype(jnp.int32)

    n_zh = lax.axis_size("zh")
    n_c = lax.axis_size("col")
    n_x = lax.axis_size("x")
    ring_panel, moved_panel = front_exchange(panel, n_x, n_zh, n_c)

    def to_rows(blocks):
        blocks = blocks.reshape(n_zh, n_c, local_rows, part_width).transpose(0, 2, 1, 3)
        return blocks.reshape(n_zh * local_rows, n_c * part_width)

    own_panel = lax.dynamic_index_in_dim(
        to_rows(ring_panel).reshape(n_zh, local_rows, panel_width), zh_index, 0, keepdims=False
    )
    own_full = jnp.dot(
        own_panel,
        diag_inverse.T,
        precision=lax.Precision.HIGHEST,
        preferred_element_type=jnp.float32,
    )
    own_block = lax.dynamic_slice_in_dim(own_full, col_index * part_width, part_width, 1)
    chosen = jnp.dot(
        to_rows(moved_panel),
        diag_inverse.T,
        precision=lax.Precision.HIGHEST,
        preferred_element_type=jnp.float32,
    ).reshape(n_zh, local_rows, panel_width)
    gathered = lax.all_gather(chosen, ("y", "core"), axis=1, tiled=False)
    partner = gathered.reshape(local_cols, panel_width)

    product = lax.dot_general(
        own_full,
        partner,
        (((1,), (1,)), ((), ())),
        precision=lax.Precision.HIGH,
        preferred_element_type=jnp.float32,
    )
    updated = add_tiles(
        landing,
        trailing - product,
        got_values.reshape(-1, TILE_ROWS, TILE_COLS),
        tile_cols,
        tiles_dev,
    )
    return (updated, own_block)


def solution(mesh):
    n_row, n_col = mesh.devices.shape
    shape = (n_col, n_col, n_col, n_row // n_col**3, n_col)
    split = Mesh(mesh.devices.reshape(shape), ROW_AXES + ("col",))
    rows = ROW_AXES
    in_specs = (
        P(),
        P(rows, "col"),
        P(rows, "col"),
        P(rows, "col", None, None),
        P(rows, "col", None, None),
        P(rows, "col", None),
    )
    out_specs = (P(rows, "col"), P(rows, "col"))
    return jax.shard_map(
        per_device, mesh=split, in_specs=in_specs, out_specs=out_specs, check_vma=False
    )
```

```python
import functools

import jax
import jax.numpy as jnp
from jax import lax
from jax.experimental import pallas as pl
from jax.experimental.pallas import tpu as pltpu
from jax.sharding import Mesh
from jax.sharding import PartitionSpec as P

TILE_ROWS = 8
TILE_COLS = 128
CAP = 2
ROW_AXES = ("x", "zh", "y", "core")
MESH_IDS = pl.DeviceIdType.MESH


def _front_kernel(n_x, n_zh, n_c, block_ref, ring_ref, moved_ref, send_sem, recv_sem,
                  xsend_sem, xrecv_sem, local_sem):
    n = n_zh * n_c
    col = lax.axis_index("col")
    x = lax.axis_index("x")
    me = lax.axis_index("zh") * n_c + col
    right = lax.rem(me + 1, n)
    left = lax.rem(me + n - 1, n)
    is_source = x == col

    def on_ring(p):
        return {"zh": p // n_c, "col": lax.rem(p, n_c)}

    def x_peer(k):
        return {"x": lax.rem(x + k, n_x)}

    barrier = pltpu.get_barrier_semaphore()
    for other in (left, right):
        pl.semaphore_signal(barrier, 1, device_id=on_ring(other), device_id_type=MESH_IDS)

    @pl.when(is_source)
    def _():
        for k in range(1, n_x):
            pl.semaphore_signal(barrier, 1, device_id=x_peer(k), device_id_type=MESH_IDS)
        pl.semaphore_wait(barrier, 2 + n_x - 1)

    @pl.when(jnp.logical_not(is_source))
    def _():
        pl.semaphore_signal(barrier, 1, device_id={"x": col}, device_id_type=MESH_IDS)
        pl.semaphore_wait(barrier, 3)

    ring_ref[me] = block_ref[...]

    def x_copy(slot, src, k):
        return pltpu.make_async_remote_copy(
            src_ref=src,
            dst_ref=moved_ref.at[slot],
            send_sem=xsend_sem.at[slot, k - 1],
            recv_sem=xrecv_sem.at[0],
            device_id=x_peer(k),
            device_id_type=MESH_IDS,
        )

    def forward_x(slot, src):
        @pl.when(is_source)
        def _():
            for k in range(1, n_x):
                x_copy(slot, src, k).start()

    counts = (n // 2, n - 1 - n // 2)
    targets = (right, left)
    signs = (-1, 1)
    sent = ([], [])
    for step in range(max(counts) + 1):
        ready = []
        for d in range(2):
            if step > counts[d]:
                continue
            slot = lax.rem(me + signs[d] * step + n, n)
            if step > 0:
                sent[d][step - 1].wait_recv()
                ready.append(slot)
            if step < counts[d]:
                src = block_ref if step == 0 else ring_ref.at[slot]
                copy = pltpu.make_async_remote_copy(
                    src_ref=src,
                    dst_ref=ring_ref.at[slot],
                    send_sem=send_sem.at[d, step],
                    recv_sem=recv_sem.at[d, step],
                    device_id=on_ring(targets[d]),
                    device_id_type=MESH_IDS,
                )
                copy.start()
                sent[d].append(copy)
        if step == 0:
            forward_x(me, block_ref)
        for slot in ready:
            forward_x(slot, ring_ref.at[slot])
    for d in range(2):
        for copy in sent[d]:
            copy.wait_send()

    @pl.when(is_source)
    def _():
        for slot in range(n):
            for k in range(1, n_x):
                x_copy(slot, ring_ref.at[slot], k).wait_send()
        local = pltpu.make_async_copy(ring_ref, moved_ref, local_sem.at[0])
        local.start()
        local.wait()

    @pl.when(jnp.logical_not(is_source))
    def _():
        whole = pltpu.make_async_remote_copy(
            src_ref=ring_ref,
            dst_ref=moved_ref,
            send_sem=local_sem.at[0],
            recv_sem=xrecv_sem.at[0],
            device_id={"x": col},
            device_id_type=MESH_IDS,
        )
        whole.wait_recv()


def front_exchange(block, n_x, n_zh, n_c):
    n = n_zh * n_c
    steps = max(n // 2, 1)
    shape = jax.ShapeDtypeStruct((n,) + block.shape, block.dtype)
    return pl.pallas_call(
        functools.partial(_front_kernel, n_x, n_zh, n_c),
        out_shape=(shape, shape),
        in_specs=[pl.BlockSpec(memory_space=pltpu.VMEM)],
        out_specs=(pl.BlockSpec(memory_space=pltpu.VMEM), pl.BlockSpec(memory_space=pltpu.VMEM)),
        scratch_shapes=[
            pltpu.SemaphoreType.DMA((2, steps)),
            pltpu.SemaphoreType.DMA((2, steps)),
            pltpu.SemaphoreType.DMA((n, max(n_x - 1, 1))),
            pltpu.SemaphoreType.DMA((1,)),
            pltpu.SemaphoreType.DMA((1,)),
        ],
        compiler_params=pltpu.CompilerParams(collective_id=0, has_side_effects=True),
    )(block)

def _add_tiles_kernel(tile_cols, tiles_dev, ids_ref, base_ref, vals_ref, out_ref):
    out_ref[...] = base_ref[...]
    tile_rows, tile_width = vals_ref.shape[1], vals_ref.shape[2]

    def body(i, carry):
        tile = ids_ref[i]

        @pl.when(tile < tiles_dev)
        def _():
            rows = pl.ds(pl.multiple_of((tile // tile_cols) * tile_rows, tile_rows), tile_rows)
            cols = pl.ds(pl.multiple_of((tile % tile_cols) * tile_width, tile_width), tile_width)
            out_ref[rows, cols] = out_ref[rows, cols] + vals_ref[i]

        return carry

    lax.fori_loop(0, vals_ref.shape[0], body, 0, unroll=8)


def add_tiles(ids, base, vals, tile_cols, tiles_dev):
    vmem = pl.BlockSpec(memory_space=pltpu.VMEM)
    return pl.pallas_call(
        functools.partial(_add_tiles_kernel, tile_cols, tiles_dev),
        out_shape=jax.ShapeDtypeStruct(base.shape, base.dtype),
        in_specs=[pl.BlockSpec(memory_space=pltpu.SMEM), vmem, vmem],
        out_specs=vmem,
    )(ids, base, vals)

def per_device(diag_inverse, panel, trailing, agg_vals, agg_dest, agg_tile):
    row_devices = lax.axis_size(ROW_AXES)
    local_rows, local_cols = trailing.shape
    panel_width = diag_inverse.shape[0]
    part_width = panel.shape[1]
    col_index = lax.axis_index("col")
    zh_index = lax.axis_index("zh")

    tile_rows = local_rows // TILE_ROWS
    tile_cols = local_cols // TILE_COLS
    tiles_dev = tile_rows * tile_cols
    tile_values = agg_vals.reshape(agg_vals.shape[2], agg_vals.shape[3])
    targets = agg_dest.reshape(-1)
    tile_ids = agg_tile.reshape(-1)
    matches = (targets[:, None] == jnp.arange(row_devices, dtype=jnp.int32)[None, :]).astype(
        jnp.int32
    )
    earlier = jnp.cumsum(matches, axis=0) - matches
    ranks = jnp.sum(earlier * matches, axis=1)
    position = targets * CAP + ranks
    id_lanes = jnp.broadcast_to(tile_ids.astype(jnp.float32)[:, None], (tile_ids.shape[0], TILE_COLS))
    payload = jnp.concatenate([tile_values, id_lanes], axis=1)
    send = (
        jnp.zeros((row_devices * CAP, payload.shape[1]), jnp.float32)
        .at[:, tile_values.shape[1]:]
        .set(float(tiles_dev))
        .at[position]
        .set(payload)
    )
    send, panel = lax.optimization_barrier((send, panel))
    got = lax.all_to_all(send, ROW_AXES, split_axis=0, concat_axis=0, tiled=True)
    got_values = got[:, : tile_values.shape[1]]
    landing = got[:, tile_values.shape[1]].astype(jnp.int32)

    n_zh = lax.axis_size("zh")
    n_c = lax.axis_size("col")
    n_x = lax.axis_size("x")
    ring_panel, moved_panel = front_exchange(panel, n_x, n_zh, n_c)

    def to_rows(blocks):
        blocks = blocks.reshape(n_zh, n_c, local_rows, part_width).transpose(0, 2, 1, 3)
        return blocks.reshape(n_zh * local_rows, n_c * part_width)

    own_panel = lax.dynamic_index_in_dim(
        to_rows(ring_panel).reshape(n_zh, local_rows, panel_width), zh_index, 0, keepdims=False
    )
    own_full = jnp.dot(
        own_panel,
        diag_inverse.T,
        precision=lax.Precision.HIGHEST,
        preferred_element_type=jnp.float32,
    )
    own_block = lax.dynamic_slice_in_dim(own_full, col_index * part_width, part_width, 1)
    chosen = jnp.dot(
        to_rows(moved_panel),
        diag_inverse.T,
        precision=lax.Precision.HIGH,
        preferred_element_type=jnp.float32,
    ).reshape(n_zh, local_rows, panel_width)
    gathered = lax.all_gather(chosen, ("y", "core"), axis=1, tiled=False)
    partner = gathered.reshape(local_cols, panel_width)

    product = lax.dot_general(
        own_full,
        partner,
        (((1,), (1,)), ((), ())),
        precision=lax.Precision.HIGH,
        preferred_element_type=jnp.float32,
    )
    updated = add_tiles(
        landing,
        trailing - product,
        got_values.reshape(-1, TILE_ROWS, TILE_COLS),
        tile_cols,
        tiles_dev,
    )
    return (updated, own_block)


def solution(mesh):
    n_row, n_col = mesh.devices.shape
    shape = (n_col, n_col, n_col, n_row // n_col**3, n_col)
    split = Mesh(mesh.devices.reshape(shape), ROW_AXES + ("col",))
    rows = ROW_AXES
    in_specs = (
        P(),
        P(rows, "col"),
        P(rows, "col"),
        P(rows, "col", None, None),
        P(rows, "col", None, None),
        P(rows, "col", None),
    )
    out_specs = (P(rows, "col"), P(rows, "col"))
    return jax.shard_map(
        per_device, mesh=split, in_specs=in_specs, out_specs=out_specs, check_vma=False
    )
```

```python
import functools

import jax
import jax.numpy as jnp
from jax import lax
from jax.experimental import pallas as pl
from jax.experimental.pallas import tpu as pltpu
from jax.sharding import Mesh
from jax.sharding import PartitionSpec as P

TILE_ROWS = 8
TILE_COLS = 128
CAP = 2
ROW_AXES = ("x", "zh", "y", "core")
MESH_IDS = pl.DeviceIdType.MESH


def _front_kernel(n_x, n_zh, n_c, block_ref, ring_ref, moved_ref, send_sem, recv_sem,
                  xsend_sem, xrecv_sem, local_sem):
    n = n_zh * n_c
    col = lax.axis_index("col")
    x = lax.axis_index("x")
    me = lax.axis_index("zh") * n_c + col
    right = lax.rem(me + 1, n)
    left = lax.rem(me + n - 1, n)
    is_source = x == col

    def on_ring(p):
        return {"zh": p // n_c, "col": lax.rem(p, n_c)}

    def x_peer(k):
        return {"x": lax.rem(x + k, n_x)}

    barrier = pltpu.get_barrier_semaphore()
    for other in (left, right):
        pl.semaphore_signal(barrier, 1, device_id=on_ring(other), device_id_type=MESH_IDS)

    for k in (1, n_x - 1):
        pl.semaphore_signal(barrier, 1, device_id=x_peer(k), device_id_type=MESH_IDS)
    pl.semaphore_wait(barrier, 4)

    ring_ref[me] = block_ref[...]

    def x_copy(slot, src, k):
        return pltpu.make_async_remote_copy(
            src_ref=src,
            dst_ref=moved_ref.at[slot],
            send_sem=xsend_sem.at[slot, 0 if k == 1 else 1],
            recv_sem=xrecv_sem.at[0],
            device_id=x_peer(k),
            device_id_type=MESH_IDS,
        )

    def forward_x(slot, src):
        @pl.when(is_source)
        def _():
            for k in (1, n_x - 1):
                x_copy(slot, src, k).start()

    counts = (n // 2, n - 1 - n // 2)
    targets = (right, left)
    signs = (-1, 1)
    sent = ([], [])
    for step in range(max(counts) + 1):
        ready = []
        for d in range(2):
            if step > counts[d]:
                continue
            slot = lax.rem(me + signs[d] * step + n, n)
            if step > 0:
                sent[d][step - 1].wait_recv()
                ready.append(slot)
            if step < counts[d]:
                src = block_ref if step == 0 else ring_ref.at[slot]
                copy = pltpu.make_async_remote_copy(
                    src_ref=src,
                    dst_ref=ring_ref.at[slot],
                    send_sem=send_sem.at[d, step],
                    recv_sem=recv_sem.at[d, step],
                    device_id=on_ring(targets[d]),
                    device_id_type=MESH_IDS,
                )
                copy.start()
                sent[d].append(copy)
        if step == 0:
            forward_x(me, block_ref)
        for slot in ready:
            forward_x(slot, ring_ref.at[slot])
    for d in range(2):
        for copy in sent[d]:
            copy.wait_send()

    @pl.when(is_source)
    def _():
        for slot in range(n):
            for k in (1, n_x - 1):
                x_copy(slot, ring_ref.at[slot], k).wait_send()
        local = pltpu.make_async_copy(ring_ref, moved_ref, local_sem.at[0])
        local.start()
        local.wait()

    shift = lax.rem(x - col + n_x, n_x)

    @pl.when(jnp.logical_not(is_source))
    def _():
        whole = pltpu.make_async_remote_copy(
            src_ref=ring_ref,
            dst_ref=moved_ref,
            send_sem=local_sem.at[0],
            recv_sem=xrecv_sem.at[0],
            device_id={"x": col},
            device_id_type=MESH_IDS,
        )
        whole.wait_recv()

    half = n // 2
    for role, first, k in ((1, 0, 1), (n_x - 1, half, n_x - 1)):
        @pl.when(shift == role)
        def _():
            part = pl.ds(first, half)
            onward = pltpu.make_async_remote_copy(
                src_ref=moved_ref.at[part],
                dst_ref=moved_ref.at[part],
                send_sem=xsend_sem.at[0, 2],
                recv_sem=xrecv_sem.at[0],
                device_id=x_peer(k),
                device_id_type=MESH_IDS,
            )
            onward.start()
            onward.wait_send()


def front_exchange(block, n_x, n_zh, n_c):
    n = n_zh * n_c
    steps = max(n // 2, 1)
    shape = jax.ShapeDtypeStruct((n,) + block.shape, block.dtype)
    return pl.pallas_call(
        functools.partial(_front_kernel, n_x, n_zh, n_c),
        out_shape=(shape, shape),
        in_specs=[pl.BlockSpec(memory_space=pltpu.VMEM)],
        out_specs=(pl.BlockSpec(memory_space=pltpu.VMEM), pl.BlockSpec(memory_space=pltpu.VMEM)),
        scratch_shapes=[
            pltpu.SemaphoreType.DMA((2, steps)),
            pltpu.SemaphoreType.DMA((2, steps)),
            pltpu.SemaphoreType.DMA((n, max(n_x - 1, 1))),
            pltpu.SemaphoreType.DMA((1,)),
            pltpu.SemaphoreType.DMA((1,)),
        ],
        compiler_params=pltpu.CompilerParams(collective_id=0, has_side_effects=True),
    )(block)

def _add_tiles_kernel(tile_cols, tiles_dev, ids_ref, base_ref, vals_ref, out_ref):
    out_ref[...] = base_ref[...]
    tile_rows, tile_width = vals_ref.shape[1], vals_ref.shape[2]

    def body(i, carry):
        tile = ids_ref[i]

        @pl.when(tile < tiles_dev)
        def _():
            rows = pl.ds(pl.multiple_of((tile // tile_cols) * tile_rows, tile_rows), tile_rows)
            cols = pl.ds(pl.multiple_of((tile % tile_cols) * tile_width, tile_width), tile_width)
            out_ref[rows, cols] = out_ref[rows, cols] + vals_ref[i]

        return carry

    lax.fori_loop(0, vals_ref.shape[0], body, 0, unroll=8)


def add_tiles(ids, base, vals, tile_cols, tiles_dev):
    vmem = pl.BlockSpec(memory_space=pltpu.VMEM)
    return pl.pallas_call(
        functools.partial(_add_tiles_kernel, tile_cols, tiles_dev),
        out_shape=jax.ShapeDtypeStruct(base.shape, base.dtype),
        in_specs=[pl.BlockSpec(memory_space=pltpu.SMEM), vmem, vmem],
        out_specs=vmem,
    )(ids, base, vals)

def per_device(diag_inverse, panel, trailing, agg_vals, agg_dest, agg_tile):
    row_devices = lax.axis_size(ROW_AXES)
    local_rows, local_cols = trailing.shape
    panel_width = diag_inverse.shape[0]
    part_width = panel.shape[1]
    col_index = lax.axis_index("col")
    zh_index = lax.axis_index("zh")

    tile_rows = local_rows // TILE_ROWS
    tile_cols = local_cols // TILE_COLS
    tiles_dev = tile_rows * tile_cols
    tile_values = agg_vals.reshape(agg_vals.shape[2], agg_vals.shape[3])
    targets = agg_dest.reshape(-1)
    tile_ids = agg_tile.reshape(-1)
    matches = (targets[:, None] == jnp.arange(row_devices, dtype=jnp.int32)[None, :]).astype(
        jnp.int32
    )
    earlier = jnp.cumsum(matches, axis=0) - matches
    ranks = jnp.sum(earlier * matches, axis=1)
    position = targets * CAP + ranks
    id_lanes = jnp.broadcast_to(tile_ids.astype(jnp.float32)[:, None], (tile_ids.shape[0], TILE_COLS))
    payload = jnp.concatenate([tile_values, id_lanes], axis=1)
    send = (
        jnp.zeros((row_devices * CAP, payload.shape[1]), jnp.float32)
        .at[:, tile_values.shape[1]:]
        .set(float(tiles_dev))
        .at[position]
        .set(payload)
    )
    got = lax.all_to_all(send, ROW_AXES, split_axis=0, concat_axis=0, tiled=True)
    got_values = got[:, : tile_values.shape[1]]
    landing = got[:, tile_values.shape[1]].astype(jnp.int32)

    n_zh = lax.axis_size("zh")
    n_c = lax.axis_size("col")
    n_x = lax.axis_size("x")
    ring_panel, moved_panel = front_exchange(panel, n_x, n_zh, n_c)

    def to_rows(blocks):
        blocks = blocks.reshape(n_zh, n_c, local_rows, part_width).transpose(0, 2, 1, 3)
        return blocks.reshape(n_zh * local_rows, n_c * part_width)

    own_panel = lax.dynamic_index_in_dim(
        to_rows(ring_panel).reshape(n_zh, local_rows, panel_width), zh_index, 0, keepdims=False
    )
    own_full = jnp.dot(
        own_panel,
        diag_inverse.T,
        precision=lax.Precision.HIGHEST,
        preferred_element_type=jnp.float32,
    )
    own_block = lax.dynamic_slice_in_dim(own_full, col_index * part_width, part_width, 1)
    chosen = jnp.dot(
        to_rows(moved_panel),
        diag_inverse.T,
        precision=lax.Precision.HIGHEST,
        preferred_element_type=jnp.float32,
    ).reshape(n_zh, local_rows, panel_width)
    gathered = lax.all_gather(chosen, ("y", "core"), axis=1, tiled=False)
    partner = gathered.reshape(local_cols, panel_width)

    product = lax.dot_general(
        own_full,
        partner,
        (((1,), (1,)), ((), ())),
        precision=lax.Precision.HIGH,
        preferred_element_type=jnp.float32,
    )
    updated = add_tiles(
        landing,
        trailing - product,
        got_values.reshape(-1, TILE_ROWS, TILE_COLS),
        tile_cols,
        tiles_dev,
    )
    return (updated, own_block)


def solution(mesh):
    n_row, n_col = mesh.devices.shape
    shape = (n_col, n_col, n_col, n_row // n_col**3, n_col)
    split = Mesh(mesh.devices.reshape(shape), ROW_AXES + ("col",))
    rows = ROW_AXES
    in_specs = (
        P(),
        P(rows, "col"),
        P(rows, "col"),
        P(rows, "col", None, None),
        P(rows, "col", None, None),
        P(rows, "col", None),
    )
    out_specs = (P(rows, "col"), P(rows, "col"))
    return jax.shard_map(
        per_device, mesh=split, in_specs=in_specs, out_specs=out_specs, check_vma=False
    )
```

```python
import functools

import jax
import jax.numpy as jnp
from jax import lax
from jax.experimental import pallas as pl
from jax.experimental.pallas import tpu as pltpu
from jax.sharding import Mesh
from jax.sharding import PartitionSpec as P

TILE_ROWS = 8
TILE_COLS = 128
CAP = 2
ROW_AXES = ("x", "zh", "y", "core")
MESH_IDS = pl.DeviceIdType.MESH


def _front_kernel(n_x, n_zh, n_c, block_ref, ring_ref, moved_ref, send_sem, recv_sem,
                  xsend_sem, xrecv_sem, local_sem):
    n = n_zh * n_c
    col = lax.axis_index("col")
    x = lax.axis_index("x")
    me = lax.axis_index("zh") * n_c + col
    right = lax.rem(me + 1, n)
    left = lax.rem(me + n - 1, n)
    is_source = x == col

    def on_ring(p):
        return {"zh": p // n_c, "col": lax.rem(p, n_c)}

    def x_peer(k):
        return {"x": lax.rem(x + k, n_x)}

    barrier = pltpu.get_barrier_semaphore()
    for other in (left, right):
        pl.semaphore_signal(barrier, 1, device_id=on_ring(other), device_id_type=MESH_IDS)

    for k in (1, n_x - 1):
        pl.semaphore_signal(barrier, 1, device_id=x_peer(k), device_id_type=MESH_IDS)
    pl.semaphore_wait(barrier, 4)

    ring_ref[me] = block_ref[...]

    def x_copy(slot, src, k):
        return pltpu.make_async_remote_copy(
            src_ref=src,
            dst_ref=moved_ref.at[slot],
            send_sem=xsend_sem.at[slot, 0 if k == 1 else 1],
            recv_sem=xrecv_sem.at[0],
            device_id=x_peer(k),
            device_id_type=MESH_IDS,
        )

    def forward_x(slot, src):
        @pl.when(is_source)
        def _():
            for k in (1, n_x - 1):
                x_copy(slot, src, k).start()

    counts = (n // 2, n - 1 - n // 2)
    targets = (right, left)
    signs = (-1, 1)
    sent = ([], [])
    for step in range(max(counts) + 1):
        ready = []
        for d in range(2):
            if step > counts[d]:
                continue
            slot = lax.rem(me + signs[d] * step + n, n)
            if step > 0:
                sent[d][step - 1].wait_recv()
                ready.append(slot)
            if step < counts[d]:
                src = block_ref if step == 0 else ring_ref.at[slot]
                copy = pltpu.make_async_remote_copy(
                    src_ref=src,
                    dst_ref=ring_ref.at[slot],
                    send_sem=send_sem.at[d, step],
                    recv_sem=recv_sem.at[d, step],
                    device_id=on_ring(targets[d]),
                    device_id_type=MESH_IDS,
                )
                copy.start()
                sent[d].append(copy)
        if step == 0:
            forward_x(me, block_ref)
        for slot in ready:
            forward_x(slot, ring_ref.at[slot])
    for d in range(2):
        for copy in sent[d]:
            copy.wait_send()

    @pl.when(is_source)
    def _():
        for slot in range(n):
            for k in (1, n_x - 1):
                x_copy(slot, ring_ref.at[slot], k).wait_send()
        local = pltpu.make_async_copy(ring_ref, moved_ref, local_sem.at[0])
        local.start()
        local.wait()

    shift = lax.rem(x - col + n_x, n_x)

    @pl.when(jnp.logical_not(is_source))
    def _():
        whole = pltpu.make_async_remote_copy(
            src_ref=ring_ref,
            dst_ref=moved_ref,
            send_sem=local_sem.at[0],
            recv_sem=xrecv_sem.at[0],
            device_id={"x": col},
            device_id_type=MESH_IDS,
        )
        whole.wait_recv()

    half = n // 2
    for role, first, k in ((1, 0, 1), (n_x - 1, half, n_x - 1)):
        @pl.when(shift == role)
        def _():
            part = pl.ds(first, half)
            onward = pltpu.make_async_remote_copy(
                src_ref=moved_ref.at[part],
                dst_ref=moved_ref.at[part],
                send_sem=xsend_sem.at[0, 2],
                recv_sem=xrecv_sem.at[0],
                device_id=x_peer(k),
                device_id_type=MESH_IDS,
            )
            onward.start()
            onward.wait_send()


def front_exchange(block, n_x, n_zh, n_c):
    n = n_zh * n_c
    steps = max(n // 2, 1)
    shape = jax.ShapeDtypeStruct((n,) + block.shape, block.dtype)
    return pl.pallas_call(
        functools.partial(_front_kernel, n_x, n_zh, n_c),
        out_shape=(shape, shape),
        in_specs=[pl.BlockSpec(memory_space=pltpu.VMEM)],
        out_specs=(pl.BlockSpec(memory_space=pltpu.VMEM), pl.BlockSpec(memory_space=pltpu.VMEM)),
        scratch_shapes=[
            pltpu.SemaphoreType.DMA((2, steps)),
            pltpu.SemaphoreType.DMA((2, steps)),
            pltpu.SemaphoreType.DMA((n, max(n_x - 1, 1))),
            pltpu.SemaphoreType.DMA((1,)),
            pltpu.SemaphoreType.DMA((1,)),
        ],
        compiler_params=pltpu.CompilerParams(collective_id=0, has_side_effects=True),
    )(block)

def _add_tiles_kernel(tile_cols, tiles_dev, ids_ref, base_ref, vals_ref, out_ref):
    out_ref[...] = base_ref[...]
    tile_rows, tile_width = vals_ref.shape[1], vals_ref.shape[2]

    def body(i, carry):
        tile = ids_ref[i]

        @pl.when(tile < tiles_dev)
        def _():
            rows = pl.ds(pl.multiple_of((tile // tile_cols) * tile_rows, tile_rows), tile_rows)
            cols = pl.ds(pl.multiple_of((tile % tile_cols) * tile_width, tile_width), tile_width)
            out_ref[rows, cols] = out_ref[rows, cols] + vals_ref[i]

        return carry

    lax.fori_loop(0, vals_ref.shape[0], body, 0, unroll=8)


def add_tiles(ids, base, vals, tile_cols, tiles_dev):
    vmem = pl.BlockSpec(memory_space=pltpu.VMEM)
    return pl.pallas_call(
        functools.partial(_add_tiles_kernel, tile_cols, tiles_dev),
        out_shape=jax.ShapeDtypeStruct(base.shape, base.dtype),
        in_specs=[pl.BlockSpec(memory_space=pltpu.SMEM), vmem, vmem],
        out_specs=vmem,
    )(ids, base, vals)

def per_device(diag_inverse, panel, trailing, agg_vals, agg_dest, agg_tile):
    row_devices = lax.axis_size(ROW_AXES)
    local_rows, local_cols = trailing.shape
    panel_width = diag_inverse.shape[0]
    part_width = panel.shape[1]
    col_index = lax.axis_index("col")
    zh_index = lax.axis_index("zh")

    tile_rows = local_rows // TILE_ROWS
    tile_cols = local_cols // TILE_COLS
    tiles_dev = tile_rows * tile_cols
    tile_values = agg_vals.reshape(agg_vals.shape[2], agg_vals.shape[3])
    targets = agg_dest.reshape(-1)
    tile_ids = agg_tile.reshape(-1)
    matches = (targets[:, None] == jnp.arange(row_devices, dtype=jnp.int32)[None, :]).astype(
        jnp.int32
    )
    earlier = jnp.cumsum(matches, axis=0) - matches
    ranks = jnp.sum(earlier * matches, axis=1)
    position = targets * CAP + ranks
    id_lanes = jnp.broadcast_to(tile_ids.astype(jnp.float32)[:, None], (tile_ids.shape[0], TILE_COLS))
    payload = jnp.concatenate([tile_values, id_lanes], axis=1)
    send = (
        jnp.zeros((row_devices * CAP, payload.shape[1]), jnp.float32)
        .at[:, tile_values.shape[1]:]
        .set(float(tiles_dev))
        .at[position]
        .set(payload)
    )
    got = lax.all_to_all(send, ROW_AXES, split_axis=0, concat_axis=0, tiled=True)
    got_values = got[:, : tile_values.shape[1]]
    landing = got[:, tile_values.shape[1]].astype(jnp.int32)

    n_zh = lax.axis_size("zh")
    n_c = lax.axis_size("col")
    n_x = lax.axis_size("x")
    ring_panel, moved_panel = front_exchange(panel, n_x, n_zh, n_c)

    def to_rows(blocks):
        blocks = blocks.reshape(n_zh, n_c, local_rows, part_width).transpose(0, 2, 1, 3)
        return blocks.reshape(n_zh * local_rows, n_c * part_width)

    own_panel = lax.dynamic_index_in_dim(
        to_rows(ring_panel).reshape(n_zh, local_rows, panel_width), zh_index, 0, keepdims=False
    )
    own_full = jnp.dot(
        own_panel,
        diag_inverse.T,
        precision=lax.Precision.HIGHEST,
        preferred_element_type=jnp.float32,
    )
    own_block = lax.dynamic_slice_in_dim(own_full, col_index * part_width, part_width, 1)
    chosen = jnp.dot(
        to_rows(moved_panel),
        diag_inverse.T,
        precision=lax.Precision.HIGH,
        preferred_element_type=jnp.float32,
    ).reshape(n_zh, local_rows, panel_width)
    gathered = lax.all_gather(chosen, ("y", "core"), axis=1, tiled=False)
    partner = gathered.reshape(local_cols, panel_width)

    product = lax.dot_general(
        own_full,
        partner,
        (((1,), (1,)), ((), ())),
        precision=lax.Precision.HIGH,
        preferred_element_type=jnp.float32,
    )
    updated = add_tiles(
        landing,
        trailing - product,
        got_values.reshape(-1, TILE_ROWS, TILE_COLS),
        tile_cols,
        tiles_dev,
    )
    return (updated, own_block)


def solution(mesh):
    n_row, n_col = mesh.devices.shape
    shape = (n_col, n_col, n_col, n_row // n_col**3, n_col)
    split = Mesh(mesh.devices.reshape(shape), ROW_AXES + ("col",))
    rows = ROW_AXES
    in_specs = (
        P(),
        P(rows, "col"),
        P(rows, "col"),
        P(rows, "col", None, None),
        P(rows, "col", None, None),
        P(rows, "col", None),
    )
    out_specs = (P(rows, "col"), P(rows, "col"))
    return jax.shard_map(
        per_device, mesh=split, in_specs=in_specs, out_specs=out_specs, check_vma=False
    )
```

```python
import functools

import jax
import jax.numpy as jnp
from jax import lax
from jax.experimental import pallas as pl
from jax.experimental.pallas import tpu as pltpu
from jax.sharding import Mesh
from jax.sharding import PartitionSpec as P

TILE_ROWS = 8
TILE_COLS = 128
CAP = 2
ROW_AXES = ("x", "zh", "y", "core")
MESH_IDS = pl.DeviceIdType.MESH


def _front_kernel(n_x, n_zh, n_c, block_ref, ring_ref, moved_ref, send_sem, recv_sem,
                  xsend_sem, xrecv_sem, local_sem):
    n = n_zh * n_c
    col = lax.axis_index("col")
    x = lax.axis_index("x")
    me = lax.axis_index("zh") * n_c + col
    right = lax.rem(me + 1, n)
    left = lax.rem(me + n - 1, n)
    is_source = x == col

    def on_ring(p):
        return {"zh": p // n_c, "col": lax.rem(p, n_c)}

    def x_peer(k):
        return {"x": lax.rem(x + k, n_x)}

    barrier = pltpu.get_barrier_semaphore()
    for other in (left, right):
        pl.semaphore_signal(barrier, 1, device_id=on_ring(other), device_id_type=MESH_IDS)

    for k in (1, n_x - 1):
        pl.semaphore_signal(barrier, 1, device_id=x_peer(k), device_id_type=MESH_IDS)
    pl.semaphore_wait(barrier, 4)

    ring_ref[me] = block_ref[...]

    def x_copy(slot, src, k):
        return pltpu.make_async_remote_copy(
            src_ref=src,
            dst_ref=moved_ref.at[slot],
            send_sem=xsend_sem.at[slot, 0 if k == 1 else 1],
            recv_sem=xrecv_sem.at[0],
            device_id=x_peer(k),
            device_id_type=MESH_IDS,
        )

    def forward_x(slot, src):
        @pl.when(is_source)
        def _():
            for k in (1, n_x - 1):
                x_copy(slot, src, k).start()

    counts = (n // 2, n - 1 - n // 2)
    targets = (right, left)
    signs = (-1, 1)
    sent = ([], [])
    for step in range(max(counts) + 1):
        ready = []
        for d in range(2):
            if step > counts[d]:
                continue
            slot = lax.rem(me + signs[d] * step + n, n)
            if step > 0:
                sent[d][step - 1].wait_recv()
                ready.append(slot)
            if step < counts[d]:
                src = block_ref if step == 0 else ring_ref.at[slot]
                copy = pltpu.make_async_remote_copy(
                    src_ref=src,
                    dst_ref=ring_ref.at[slot],
                    send_sem=send_sem.at[d, step],
                    recv_sem=recv_sem.at[d, step],
                    device_id=on_ring(targets[d]),
                    device_id_type=MESH_IDS,
                )
                copy.start()
                sent[d].append(copy)
        if step == 0:
            forward_x(me, block_ref)
        for slot in ready:
            forward_x(slot, ring_ref.at[slot])
    for d in range(2):
        for copy in sent[d]:
            copy.wait_send()

    @pl.when(is_source)
    def _():
        for slot in range(n):
            for k in (1, n_x - 1):
                x_copy(slot, ring_ref.at[slot], k).wait_send()
        local = pltpu.make_async_copy(ring_ref, moved_ref, local_sem.at[0])
        local.start()
        local.wait()

    shift = lax.rem(x - col + n_x, n_x)

    @pl.when(jnp.logical_not(is_source))
    def _():
        whole = pltpu.make_async_remote_copy(
            src_ref=ring_ref,
            dst_ref=moved_ref,
            send_sem=local_sem.at[0],
            recv_sem=xrecv_sem.at[0],
            device_id={"x": col},
            device_id_type=MESH_IDS,
        )
        whole.wait_recv()

    half = n // 2
    for role, first, k in ((1, 0, 1), (n_x - 1, half, n_x - 1)):
        @pl.when(shift == role)
        def _():
            part = pl.ds(first, half)
            onward = pltpu.make_async_remote_copy(
                src_ref=moved_ref.at[part],
                dst_ref=moved_ref.at[part],
                send_sem=xsend_sem.at[0, 2],
                recv_sem=xrecv_sem.at[0],
                device_id=x_peer(k),
                device_id_type=MESH_IDS,
            )
            onward.start()
            onward.wait_send()


def front_exchange(block, n_x, n_zh, n_c):
    n = n_zh * n_c
    steps = max(n // 2, 1)
    shape = jax.ShapeDtypeStruct((n,) + block.shape, block.dtype)
    return pl.pallas_call(
        functools.partial(_front_kernel, n_x, n_zh, n_c),
        out_shape=(shape, shape),
        in_specs=[pl.BlockSpec(memory_space=pltpu.VMEM)],
        out_specs=(pl.BlockSpec(memory_space=pltpu.VMEM), pl.BlockSpec(memory_space=pltpu.VMEM)),
        scratch_shapes=[
            pltpu.SemaphoreType.DMA((2, steps)),
            pltpu.SemaphoreType.DMA((2, steps)),
            pltpu.SemaphoreType.DMA((n, max(n_x - 1, 1))),
            pltpu.SemaphoreType.DMA((1,)),
            pltpu.SemaphoreType.DMA((1,)),
        ],
        compiler_params=pltpu.CompilerParams(collective_id=0, has_side_effects=True),
    )(block)

def _add_tiles_kernel(tile_cols, tiles_dev, ids_ref, base_ref, vals_ref, out_ref):
    out_ref[...] = base_ref[...]
    tile_rows, tile_width = vals_ref.shape[1], vals_ref.shape[2]

    def body(i, carry):
        tile = ids_ref[i]

        @pl.when(tile < tiles_dev)
        def _():
            rows = pl.ds(pl.multiple_of((tile // tile_cols) * tile_rows, tile_rows), tile_rows)
            cols = pl.ds(pl.multiple_of((tile % tile_cols) * tile_width, tile_width), tile_width)
            out_ref[rows, cols] = out_ref[rows, cols] + vals_ref[i]

        return carry

    lax.fori_loop(0, vals_ref.shape[0], body, 0, unroll=8)


def add_tiles(ids, base, vals, tile_cols, tiles_dev):
    vmem = pl.BlockSpec(memory_space=pltpu.VMEM)
    return pl.pallas_call(
        functools.partial(_add_tiles_kernel, tile_cols, tiles_dev),
        out_shape=jax.ShapeDtypeStruct(base.shape, base.dtype),
        in_specs=[pl.BlockSpec(memory_space=pltpu.SMEM), vmem, vmem],
        out_specs=vmem,
    )(ids, base, vals)

def per_device(diag_inverse, panel, trailing, agg_vals, agg_dest, agg_tile):
    row_devices = lax.axis_size(ROW_AXES)
    local_rows, local_cols = trailing.shape
    panel_width = diag_inverse.shape[0]
    part_width = panel.shape[1]
    col_index = lax.axis_index("col")
    zh_index = lax.axis_index("zh")

    tile_rows = local_rows // TILE_ROWS
    tile_cols = local_cols // TILE_COLS
    tiles_dev = tile_rows * tile_cols
    tile_values = agg_vals.reshape(agg_vals.shape[2], agg_vals.shape[3])
    targets = agg_dest.reshape(-1)
    tile_ids = agg_tile.reshape(-1)
    matches = (targets[:, None] == jnp.arange(row_devices, dtype=jnp.int32)[None, :]).astype(
        jnp.int32
    )
    earlier = jnp.cumsum(matches, axis=0) - matches
    ranks = jnp.sum(earlier * matches, axis=1)
    position = targets * CAP + ranks
    id_lanes = jnp.broadcast_to(tile_ids.astype(jnp.float32)[:, None], (tile_ids.shape[0], TILE_COLS))
    payload = jnp.concatenate([tile_values, id_lanes], axis=1)
    send = (
        jnp.zeros((row_devices, CAP, payload.shape[1]), jnp.float32)
        .at[:, :, tile_values.shape[1]:]
        .set(float(tiles_dev))
        .at[targets, ranks]
        .set(payload)
    )
    send, panel = lax.optimization_barrier((send, panel))
    got = lax.all_to_all(send, ROW_AXES, split_axis=0, concat_axis=0, tiled=True)
    got = got.reshape(row_devices * CAP, payload.shape[1])
    got_values = got[:, : tile_values.shape[1]]
    landing = got[:, tile_values.shape[1]].astype(jnp.int32)

    n_zh = lax.axis_size("zh")
    n_c = lax.axis_size("col")
    n_x = lax.axis_size("x")
    ring_panel, moved_panel = front_exchange(panel, n_x, n_zh, n_c)

    def to_rows(blocks):
        blocks = blocks.reshape(n_zh, n_c, local_rows, part_width).transpose(0, 2, 1, 3)
        return blocks.reshape(n_zh * local_rows, n_c * part_width)

    own_panel = lax.dynamic_index_in_dim(
        to_rows(ring_panel).reshape(n_zh, local_rows, panel_width), zh_index, 0, keepdims=False
    )
    own_full = jnp.dot(
        own_panel,
        diag_inverse.T,
        precision=lax.Precision.HIGHEST,
        preferred_element_type=jnp.float32,
    )
    own_block = lax.dynamic_slice_in_dim(own_full, col_index * part_width, part_width, 1)
    chosen = jnp.dot(
        to_rows(moved_panel),
        diag_inverse.T,
        precision=lax.Precision.HIGHEST,
        preferred_element_type=jnp.float32,
    ).reshape(n_zh, local_rows, panel_width)
    gathered = lax.all_gather(chosen, ("y", "core"), axis=1, tiled=False)
    partner = gathered.reshape(local_cols, panel_width)

    product = lax.dot_general(
        own_full,
        partner,
        (((1,), (1,)), ((), ())),
        precision=lax.Precision.HIGH,
        preferred_element_type=jnp.float32,
    )
    updated = add_tiles(
        landing,
        trailing - product,
        got_values.reshape(-1, TILE_ROWS, TILE_COLS),
        tile_cols,
        tiles_dev,
    )
    return (updated, own_block)


def solution(mesh):
    n_row, n_col = mesh.devices.shape
    shape = (n_col, n_col, n_col, n_row // n_col**3, n_col)
    split = Mesh(mesh.devices.reshape(shape), ROW_AXES + ("col",))
    rows = ROW_AXES
    in_specs = (
        P(),
        P(rows, "col"),
        P(rows, "col"),
        P(rows, "col", None, None),
        P(rows, "col", None, None),
        P(rows, "col", None),
    )
    out_specs = (P(rows, "col"), P(rows, "col"))
    return jax.shard_map(
        per_device, mesh=split, in_specs=in_specs, out_specs=out_specs, check_vma=False
    )
```

```python
import functools

import jax
import jax.numpy as jnp
from jax import lax
from jax.experimental import pallas as pl
from jax.experimental.pallas import tpu as pltpu
from jax.sharding import Mesh
from jax.sharding import PartitionSpec as P

TILE_ROWS = 8
TILE_COLS = 128
CAP = 2
ROW_AXES = ("x", "zh", "y", "core")
MESH_IDS = pl.DeviceIdType.MESH


def _front_kernel(n_x, n_zh, n_c, block_ref, ring_ref, moved_ref, send_sem, recv_sem,
                  xsend_sem, xrecv_sem, local_sem):
    n = n_zh * n_c
    col = lax.axis_index("col")
    x = lax.axis_index("x")
    me = lax.axis_index("zh") * n_c + col
    right = lax.rem(me + 1, n)
    left = lax.rem(me + n - 1, n)
    is_source = x == col

    def on_ring(p):
        return {"zh": p // n_c, "col": lax.rem(p, n_c)}

    def x_peer(k):
        return {"x": lax.rem(x + k, n_x)}

    barrier = pltpu.get_barrier_semaphore()
    for other in (left, right):
        pl.semaphore_signal(barrier, 1, device_id=on_ring(other), device_id_type=MESH_IDS)

    for k in (1, n_x - 1):
        pl.semaphore_signal(barrier, 1, device_id=x_peer(k), device_id_type=MESH_IDS)
    pl.semaphore_wait(barrier, 4)

    ring_ref[me] = block_ref[...]

    def x_copy(slot, src, k):
        return pltpu.make_async_remote_copy(
            src_ref=src,
            dst_ref=moved_ref.at[slot],
            send_sem=xsend_sem.at[slot, 0 if k == 1 else 1],
            recv_sem=xrecv_sem.at[0],
            device_id=x_peer(k),
            device_id_type=MESH_IDS,
        )

    def forward_x(slot, src):
        @pl.when(is_source)
        def _():
            for k in (1, n_x - 1):
                x_copy(slot, src, k).start()

    counts = (n // 2, n - 1 - n // 2)
    targets = (right, left)
    signs = (-1, 1)
    sent = ([], [])
    for step in range(max(counts) + 1):
        ready = []
        for d in range(2):
            if step > counts[d]:
                continue
            slot = lax.rem(me + signs[d] * step + n, n)
            if step > 0:
                sent[d][step - 1].wait_recv()
                ready.append(slot)
            if step < counts[d]:
                src = block_ref if step == 0 else ring_ref.at[slot]
                copy = pltpu.make_async_remote_copy(
                    src_ref=src,
                    dst_ref=ring_ref.at[slot],
                    send_sem=send_sem.at[d, step],
                    recv_sem=recv_sem.at[d, step],
                    device_id=on_ring(targets[d]),
                    device_id_type=MESH_IDS,
                )
                copy.start()
                sent[d].append(copy)
        if step == 0:
            forward_x(me, block_ref)
        for slot in ready:
            forward_x(slot, ring_ref.at[slot])
    for d in range(2):
        for copy in sent[d]:
            copy.wait_send()

    @pl.when(is_source)
    def _():
        for slot in range(n):
            for k in (1, n_x - 1):
                x_copy(slot, ring_ref.at[slot], k).wait_send()
        local = pltpu.make_async_copy(ring_ref, moved_ref, local_sem.at[0])
        local.start()
        local.wait()

    shift = lax.rem(x - col + n_x, n_x)

    @pl.when(jnp.logical_not(is_source))
    def _():
        whole = pltpu.make_async_remote_copy(
            src_ref=ring_ref,
            dst_ref=moved_ref,
            send_sem=local_sem.at[0],
            recv_sem=xrecv_sem.at[0],
            device_id={"x": col},
            device_id_type=MESH_IDS,
        )
        whole.wait_recv()

    half = n // 2
    for role, first, k in ((1, 0, 1), (n_x - 1, half, n_x - 1)):
        @pl.when(shift == role)
        def _():
            part = pl.ds(first, half)
            onward = pltpu.make_async_remote_copy(
                src_ref=moved_ref.at[part],
                dst_ref=moved_ref.at[part],
                send_sem=xsend_sem.at[0, 2],
                recv_sem=xrecv_sem.at[0],
                device_id=x_peer(k),
                device_id_type=MESH_IDS,
            )
            onward.start()
            onward.wait_send()


def front_exchange(block, n_x, n_zh, n_c):
    n = n_zh * n_c
    steps = max(n // 2, 1)
    shape = jax.ShapeDtypeStruct((n,) + block.shape, block.dtype)
    return pl.pallas_call(
        functools.partial(_front_kernel, n_x, n_zh, n_c),
        out_shape=(shape, shape),
        in_specs=[pl.BlockSpec(memory_space=pltpu.VMEM)],
        out_specs=(pl.BlockSpec(memory_space=pltpu.VMEM), pl.BlockSpec(memory_space=pltpu.VMEM)),
        scratch_shapes=[
            pltpu.SemaphoreType.DMA((2, steps)),
            pltpu.SemaphoreType.DMA((2, steps)),
            pltpu.SemaphoreType.DMA((n, max(n_x - 1, 1))),
            pltpu.SemaphoreType.DMA((1,)),
            pltpu.SemaphoreType.DMA((1,)),
        ],
        compiler_params=pltpu.CompilerParams(collective_id=0, has_side_effects=True),
    )(block)

def _add_tiles_kernel(tile_cols, tiles_dev, ids_ref, base_ref, vals_ref, out_ref):
    out_ref[...] = base_ref[...]
    tile_rows, tile_width = vals_ref.shape[1], vals_ref.shape[2]

    def body(i, carry):
        tile = ids_ref[i]

        @pl.when(tile < tiles_dev)
        def _():
            rows = pl.ds(pl.multiple_of((tile // tile_cols) * tile_rows, tile_rows), tile_rows)
            cols = pl.ds(pl.multiple_of((tile % tile_cols) * tile_width, tile_width), tile_width)
            out_ref[rows, cols] = out_ref[rows, cols] + vals_ref[i]

        return carry

    lax.fori_loop(0, vals_ref.shape[0], body, 0, unroll=8)


def add_tiles(ids, base, vals, tile_cols, tiles_dev):
    vmem = pl.BlockSpec(memory_space=pltpu.VMEM)
    return pl.pallas_call(
        functools.partial(_add_tiles_kernel, tile_cols, tiles_dev),
        out_shape=jax.ShapeDtypeStruct(base.shape, base.dtype),
        in_specs=[pl.BlockSpec(memory_space=pltpu.SMEM), vmem, vmem],
        out_specs=vmem,
    )(ids, base, vals)

def per_device(diag_inverse, panel, trailing, agg_vals, agg_dest, agg_tile):
    row_devices = lax.axis_size(ROW_AXES)
    local_rows, local_cols = trailing.shape
    panel_width = diag_inverse.shape[0]
    part_width = panel.shape[1]
    col_index = lax.axis_index("col")
    zh_index = lax.axis_index("zh")

    tile_rows = local_rows // TILE_ROWS
    tile_cols = local_cols // TILE_COLS
    tiles_dev = tile_rows * tile_cols
    tile_values = agg_vals.reshape(agg_vals.shape[2], agg_vals.shape[3])
    targets = agg_dest.reshape(-1)
    tile_ids = agg_tile.reshape(-1)
    matches = (targets[:, None] == jnp.arange(row_devices, dtype=jnp.int32)[None, :]).astype(
        jnp.int32
    )
    earlier = jnp.cumsum(matches, axis=0) - matches
    ranks = jnp.sum(earlier * matches, axis=1)
    position = targets * CAP + ranks
    id_lanes = jnp.broadcast_to(tile_ids.astype(jnp.float32)[:, None], (tile_ids.shape[0], TILE_COLS))
    payload = jnp.concatenate([tile_values, id_lanes], axis=1)
    send = (
        jnp.zeros((row_devices * CAP, payload.shape[1]), jnp.float32)
        .at[:, tile_values.shape[1]:]
        .set(float(tiles_dev))
        .at[position]
        .set(payload)
    )
    send = send.reshape(row_devices, CAP, payload.shape[1])
    send, panel = lax.optimization_barrier((send, panel))
    got = lax.all_to_all(send, ROW_AXES, split_axis=0, concat_axis=0, tiled=True)
    got = got.reshape(row_devices * CAP, payload.shape[1])
    got_values = got[:, : tile_values.shape[1]]
    landing = got[:, tile_values.shape[1]].astype(jnp.int32)

    n_zh = lax.axis_size("zh")
    n_c = lax.axis_size("col")
    n_x = lax.axis_size("x")
    ring_panel, moved_panel = front_exchange(panel, n_x, n_zh, n_c)

    def to_rows(blocks):
        blocks = blocks.reshape(n_zh, n_c, local_rows, part_width).transpose(0, 2, 1, 3)
        return blocks.reshape(n_zh * local_rows, n_c * part_width)

    own_panel = lax.dynamic_index_in_dim(
        to_rows(ring_panel).reshape(n_zh, local_rows, panel_width), zh_index, 0, keepdims=False
    )
    own_full = jnp.dot(
        own_panel,
        diag_inverse.T,
        precision=lax.Precision.HIGHEST,
        preferred_element_type=jnp.float32,
    )
    own_block = lax.dynamic_slice_in_dim(own_full, col_index * part_width, part_width, 1)
    chosen = jnp.dot(
        to_rows(moved_panel),
        diag_inverse.T,
        precision=lax.Precision.HIGHEST,
        preferred_element_type=jnp.float32,
    ).reshape(n_zh, local_rows, panel_width)
    gathered = lax.all_gather(chosen, ("y", "core"), axis=1, tiled=False)
    partner = gathered.reshape(local_cols, panel_width)

    product = lax.dot_general(
        own_full,
        partner,
        (((1,), (1,)), ((), ())),
        precision=lax.Precision.HIGH,
        preferred_element_type=jnp.float32,
    )
    updated = add_tiles(
        landing,
        trailing - product,
        got_values.reshape(-1, TILE_ROWS, TILE_COLS),
        tile_cols,
        tiles_dev,
    )
    return (updated, own_block)


def solution(mesh):
    n_row, n_col = mesh.devices.shape
    shape = (n_col, n_col, n_col, n_row // n_col**3, n_col)
    split = Mesh(mesh.devices.reshape(shape), ROW_AXES + ("col",))
    rows = ROW_AXES
    in_specs = (
        P(),
        P(rows, "col"),
        P(rows, "col"),
        P(rows, "col", None, None),
        P(rows, "col", None, None),
        P(rows, "col", None),
    )
    out_specs = (P(rows, "col"), P(rows, "col"))
    return jax.shard_map(
        per_device, mesh=split, in_specs=in_specs, out_specs=out_specs, check_vma=False
    )
```

```python
import functools

import jax
import jax.numpy as jnp
from jax import lax
from jax.experimental import pallas as pl
from jax.experimental.pallas import tpu as pltpu
from jax.sharding import Mesh
from jax.sharding import PartitionSpec as P

TILE_ROWS = 8
TILE_COLS = 128
CAP = 2
ROW_AXES = ("x", "zh", "y", "core")
MESH_IDS = pl.DeviceIdType.MESH


def _front_kernel(n_x, n_zh, n_c, block_ref, ring_ref, moved_ref, send_sem, recv_sem,
                  xsend_sem, xrecv_sem, local_sem):
    n = n_zh * n_c
    col = lax.axis_index("col")
    x = lax.axis_index("x")
    me = lax.axis_index("zh") * n_c + col
    right = lax.rem(me + 1, n)
    left = lax.rem(me + n - 1, n)
    is_source = x == col

    def on_ring(p):
        return {"zh": p // n_c, "col": lax.rem(p, n_c)}

    def x_peer(k):
        return {"x": lax.rem(x + k, n_x)}

    barrier = pltpu.get_barrier_semaphore()
    for other in (left, right):
        pl.semaphore_signal(barrier, 1, device_id=on_ring(other), device_id_type=MESH_IDS)

    for k in (1, n_x - 1):
        pl.semaphore_signal(barrier, 1, device_id=x_peer(k), device_id_type=MESH_IDS)
    pl.semaphore_wait(barrier, 4)

    ring_ref[me] = block_ref[...]

    def x_copy(slot, src, k):
        return pltpu.make_async_remote_copy(
            src_ref=src,
            dst_ref=moved_ref.at[slot],
            send_sem=xsend_sem.at[slot, 0 if k == 1 else 1],
            recv_sem=xrecv_sem.at[0],
            device_id=x_peer(k),
            device_id_type=MESH_IDS,
        )

    def forward_x(slot, src):
        @pl.when(is_source)
        def _():
            for k in (1, n_x - 1):
                x_copy(slot, src, k).start()

    counts = (n // 2, n - 1 - n // 2)
    targets = (right, left)
    signs = (-1, 1)
    sent = ([], [])
    for step in range(max(counts) + 1):
        ready = []
        for d in range(2):
            if step > counts[d]:
                continue
            slot = lax.rem(me + signs[d] * step + n, n)
            if step > 0:
                sent[d][step - 1].wait_recv()
                ready.append(slot)
            if step < counts[d]:
                src = block_ref if step == 0 else ring_ref.at[slot]
                copy = pltpu.make_async_remote_copy(
                    src_ref=src,
                    dst_ref=ring_ref.at[slot],
                    send_sem=send_sem.at[d, step],
                    recv_sem=recv_sem.at[d, step],
                    device_id=on_ring(targets[d]),
                    device_id_type=MESH_IDS,
                )
                copy.start()
                sent[d].append(copy)
        if step == 0:
            forward_x(me, block_ref)
        for slot in ready:
            forward_x(slot, ring_ref.at[slot])
    for d in range(2):
        for copy in sent[d]:
            copy.wait_send()

    @pl.when(is_source)
    def _():
        for slot in range(n):
            for k in (1, n_x - 1):
                x_copy(slot, ring_ref.at[slot], k).wait_send()
        local = pltpu.make_async_copy(ring_ref, moved_ref, local_sem.at[0])
        local.start()
        local.wait()

    shift = lax.rem(x - col + n_x, n_x)

    @pl.when(jnp.logical_not(is_source))
    def _():
        whole = pltpu.make_async_remote_copy(
            src_ref=ring_ref,
            dst_ref=moved_ref,
            send_sem=local_sem.at[0],
            recv_sem=xrecv_sem.at[0],
            device_id={"x": col},
            device_id_type=MESH_IDS,
        )
        whole.wait_recv()

    half = n // 2
    for role, first, k in ((1, 0, 1), (n_x - 1, half, n_x - 1)):
        @pl.when(shift == role)
        def _():
            part = pl.ds(first, half)
            onward = pltpu.make_async_remote_copy(
                src_ref=moved_ref.at[part],
                dst_ref=moved_ref.at[part],
                send_sem=xsend_sem.at[0, 2],
                recv_sem=xrecv_sem.at[0],
                device_id=x_peer(k),
                device_id_type=MESH_IDS,
            )
            onward.start()
            onward.wait_send()


def front_exchange(block, n_x, n_zh, n_c):
    n = n_zh * n_c
    steps = max(n // 2, 1)
    shape = jax.ShapeDtypeStruct((n,) + block.shape, block.dtype)
    return pl.pallas_call(
        functools.partial(_front_kernel, n_x, n_zh, n_c),
        out_shape=(shape, shape),
        in_specs=[pl.BlockSpec(memory_space=pltpu.VMEM)],
        out_specs=(pl.BlockSpec(memory_space=pltpu.VMEM), pl.BlockSpec(memory_space=pltpu.VMEM)),
        scratch_shapes=[
            pltpu.SemaphoreType.DMA((2, steps)),
            pltpu.SemaphoreType.DMA((2, steps)),
            pltpu.SemaphoreType.DMA((n, max(n_x - 1, 1))),
            pltpu.SemaphoreType.DMA((1,)),
            pltpu.SemaphoreType.DMA((1,)),
        ],
        compiler_params=pltpu.CompilerParams(collective_id=0, has_side_effects=True),
    )(block)

def _add_tiles_kernel(tile_cols, tiles_dev, ids_ref, base_ref, vals_ref, out_ref):
    out_ref[...] = base_ref[...]
    tile_rows, tile_width = vals_ref.shape[1], vals_ref.shape[2]

    def body(i, carry):
        tile = ids_ref[i]

        @pl.when(tile < tiles_dev)
        def _():
            rows = pl.ds(pl.multiple_of((tile // tile_cols) * tile_rows, tile_rows), tile_rows)
            cols = pl.ds(pl.multiple_of((tile % tile_cols) * tile_width, tile_width), tile_width)
            out_ref[rows, cols] = out_ref[rows, cols] + vals_ref[i]

        return carry

    lax.fori_loop(0, vals_ref.shape[0], body, 0, unroll=32)


def add_tiles(ids, base, vals, tile_cols, tiles_dev):
    vmem = pl.BlockSpec(memory_space=pltpu.VMEM)
    return pl.pallas_call(
        functools.partial(_add_tiles_kernel, tile_cols, tiles_dev),
        out_shape=jax.ShapeDtypeStruct(base.shape, base.dtype),
        in_specs=[pl.BlockSpec(memory_space=pltpu.SMEM), vmem, vmem],
        out_specs=vmem,
    )(ids, base, vals)

def per_device(diag_inverse, panel, trailing, agg_vals, agg_dest, agg_tile):
    row_devices = lax.axis_size(ROW_AXES)
    local_rows, local_cols = trailing.shape
    panel_width = diag_inverse.shape[0]
    part_width = panel.shape[1]
    col_index = lax.axis_index("col")
    zh_index = lax.axis_index("zh")

    tile_rows = local_rows // TILE_ROWS
    tile_cols = local_cols // TILE_COLS
    tiles_dev = tile_rows * tile_cols
    tile_values = agg_vals.reshape(agg_vals.shape[2], agg_vals.shape[3])
    targets = agg_dest.reshape(-1)
    tile_ids = agg_tile.reshape(-1)
    matches = (targets[:, None] == jnp.arange(row_devices, dtype=jnp.int32)[None, :]).astype(
        jnp.int32
    )
    earlier = jnp.cumsum(matches, axis=0) - matches
    ranks = jnp.sum(earlier * matches, axis=1)
    position = targets * CAP + ranks
    id_lanes = jnp.broadcast_to(tile_ids.astype(jnp.float32)[:, None], (tile_ids.shape[0], TILE_COLS))
    payload = jnp.concatenate([tile_values, id_lanes], axis=1)
    send = (
        jnp.zeros((row_devices * CAP, payload.shape[1]), jnp.float32)
        .at[:, tile_values.shape[1]:]
        .set(float(tiles_dev))
        .at[position]
        .set(payload)
    )
    got = lax.all_to_all(send, ROW_AXES, split_axis=0, concat_axis=0, tiled=True)
    got_values = got[:, : tile_values.shape[1]]
    landing = got[:, tile_values.shape[1]].astype(jnp.int32)

    n_zh = lax.axis_size("zh")
    n_c = lax.axis_size("col")
    n_x = lax.axis_size("x")
    ring_panel, moved_panel = front_exchange(panel, n_x, n_zh, n_c)

    def to_rows(blocks):
        blocks = blocks.reshape(n_zh, n_c, local_rows, part_width).transpose(0, 2, 1, 3)
        return blocks.reshape(n_zh * local_rows, n_c * part_width)

    own_panel = lax.dynamic_index_in_dim(
        to_rows(ring_panel).reshape(n_zh, local_rows, panel_width), zh_index, 0, keepdims=False
    )
    own_full = jnp.dot(
        own_panel,
        diag_inverse.T,
        precision=lax.Precision.HIGHEST,
        preferred_element_type=jnp.float32,
    )
    own_block = lax.dynamic_slice_in_dim(own_full, col_index * part_width, part_width, 1)
    chosen = jnp.dot(
        to_rows(moved_panel),
        diag_inverse.T,
        precision=lax.Precision.HIGHEST,
        preferred_element_type=jnp.float32,
    ).reshape(n_zh, local_rows, panel_width)
    gathered = lax.all_gather(chosen, ("y", "core"), axis=1, tiled=False)
    partner = gathered.reshape(local_cols, panel_width)

    product = lax.dot_general(
        own_full,
        partner,
        (((1,), (1,)), ((), ())),
        precision=lax.Precision.HIGH,
        preferred_element_type=jnp.float32,
    )
    updated = add_tiles(
        landing,
        trailing - product,
        got_values.reshape(-1, TILE_ROWS, TILE_COLS),
        tile_cols,
        tiles_dev,
    )
    return (updated, own_block)


def solution(mesh):
    n_row, n_col = mesh.devices.shape
    shape = (n_col, n_col, n_col, n_row // n_col**3, n_col)
    split = Mesh(mesh.devices.reshape(shape), ROW_AXES + ("col",))
    rows = ROW_AXES
    in_specs = (
        P(),
        P(rows, "col"),
        P(rows, "col"),
        P(rows, "col", None, None),
        P(rows, "col", None, None),
        P(rows, "col", None),
    )
    out_specs = (P(rows, "col"), P(rows, "col"))
    return jax.shard_map(
        per_device, mesh=split, in_specs=in_specs, out_specs=out_specs, check_vma=False
    )
```

```python
import functools

import jax
import jax.numpy as jnp
from jax import lax
from jax.experimental import pallas as pl
from jax.experimental.pallas import tpu as pltpu
from jax.sharding import Mesh
from jax.sharding import PartitionSpec as P

TILE_ROWS = 8
TILE_COLS = 128
CAP = 2
ROW_AXES = ("x", "zh", "y", "core")
MESH_IDS = pl.DeviceIdType.MESH


def _front_kernel(n_x, n_zh, n_c, block_ref, ring_ref, moved_ref, send_sem, recv_sem,
                  xsend_sem, xrecv_sem, local_sem):
    n = n_zh * n_c
    col = lax.axis_index("col")
    x = lax.axis_index("x")
    me = lax.axis_index("zh") * n_c + col
    right = lax.rem(me + 1, n)
    left = lax.rem(me + n - 1, n)
    is_source = x == col
    direct_from = n - n // 3
    relay_a = direct_from // 2

    def on_ring(p):
        return {"zh": p // n_c, "col": lax.rem(p, n_c)}

    def x_peer(k):
        return {"x": lax.rem(x + k, n_x)}

    barrier = pltpu.get_barrier_semaphore()
    for other in (left, right):
        pl.semaphore_signal(barrier, 1, device_id=on_ring(other), device_id_type=MESH_IDS)

    for k in (1, 2, n_x - 1):
        pl.semaphore_signal(barrier, 1, device_id=x_peer(k), device_id_type=MESH_IDS)
    pl.semaphore_wait(barrier, 5)

    ring_ref[me] = block_ref[...]

    def x_copy(slot, src, k):
        return pltpu.make_async_remote_copy(
            src_ref=src,
            dst_ref=moved_ref.at[slot],
            send_sem=xsend_sem.at[slot, {1: 0, 2: 2}.get(k, 1)],
            recv_sem=xrecv_sem.at[0],
            device_id=x_peer(k),
            device_id_type=MESH_IDS,
        )

    def forward_x(slot, src):
        @pl.when(is_source)
        def _():
            for k in (1, n_x - 1):
                x_copy(slot, src, k).start()

            @pl.when(slot >= direct_from)
            def _():
                x_copy(slot, src, 2).start()

    counts = (n // 2, n - 1 - n // 2)
    targets = (right, left)
    signs = (-1, 1)
    sent = ([], [])
    for step in range(max(counts) + 1):
        ready = []
        for d in range(2):
            if step > counts[d]:
                continue
            slot = lax.rem(me + signs[d] * step + n, n)
            if step > 0:
                sent[d][step - 1].wait_recv()
                ready.append(slot)
            if step < counts[d]:
                src = block_ref if step == 0 else ring_ref.at[slot]
                copy = pltpu.make_async_remote_copy(
                    src_ref=src,
                    dst_ref=ring_ref.at[slot],
                    send_sem=send_sem.at[d, step],
                    recv_sem=recv_sem.at[d, step],
                    device_id=on_ring(targets[d]),
                    device_id_type=MESH_IDS,
                )
                copy.start()
                sent[d].append(copy)
        if step == 0:
            forward_x(me, block_ref)
        for slot in ready:
            forward_x(slot, ring_ref.at[slot])
    for d in range(2):
        for copy in sent[d]:
            copy.wait_send()

    @pl.when(is_source)
    def _():
        for slot in range(n):
            for k in (1, n_x - 1):
                x_copy(slot, ring_ref.at[slot], k).wait_send()
        for slot in range(direct_from, n):
            x_copy(slot, ring_ref.at[slot], 2).wait_send()
        local = pltpu.make_async_copy(ring_ref, moved_ref, local_sem.at[0])
        local.start()
        local.wait()

    shift = lax.rem(x - col + n_x, n_x)

    @pl.when(jnp.logical_not(is_source))
    def _():
        whole = pltpu.make_async_remote_copy(
            src_ref=ring_ref,
            dst_ref=moved_ref,
            send_sem=local_sem.at[0],
            recv_sem=xrecv_sem.at[0],
            device_id={"x": col},
            device_id_type=MESH_IDS,
        )
        whole.wait_recv()

    for role, first, size, k in ((1, 0, relay_a, 1), (n_x - 1, relay_a, direct_from - relay_a, n_x - 1)):
        @pl.when(shift == role)
        def _():
            part = pl.ds(first, size)
            onward = pltpu.make_async_remote_copy(
                src_ref=moved_ref.at[part],
                dst_ref=moved_ref.at[part],
                send_sem=xsend_sem.at[0, 2],
                recv_sem=xrecv_sem.at[0],
                device_id=x_peer(k),
                device_id_type=MESH_IDS,
            )
            onward.start()
            onward.wait_send()


def front_exchange(block, n_x, n_zh, n_c):
    n = n_zh * n_c
    steps = max(n // 2, 1)
    shape = jax.ShapeDtypeStruct((n,) + block.shape, block.dtype)
    return pl.pallas_call(
        functools.partial(_front_kernel, n_x, n_zh, n_c),
        out_shape=(shape, shape),
        in_specs=[pl.BlockSpec(memory_space=pltpu.VMEM)],
        out_specs=(pl.BlockSpec(memory_space=pltpu.VMEM), pl.BlockSpec(memory_space=pltpu.VMEM)),
        scratch_shapes=[
            pltpu.SemaphoreType.DMA((2, steps)),
            pltpu.SemaphoreType.DMA((2, steps)),
            pltpu.SemaphoreType.DMA((n, max(n_x - 1, 3))),
            pltpu.SemaphoreType.DMA((1,)),
            pltpu.SemaphoreType.DMA((1,)),
        ],
        compiler_params=pltpu.CompilerParams(collective_id=0, has_side_effects=True),
    )(block)

def _add_tiles_kernel(tile_cols, tiles_dev, ids_ref, base_ref, vals_ref, out_ref):
    out_ref[...] = base_ref[...]
    tile_rows, tile_width = vals_ref.shape[1], vals_ref.shape[2]

    def body(i, carry):
        tile = ids_ref[i]

        @pl.when(tile < tiles_dev)
        def _():
            rows = pl.ds(pl.multiple_of((tile // tile_cols) * tile_rows, tile_rows), tile_rows)
            cols = pl.ds(pl.multiple_of((tile % tile_cols) * tile_width, tile_width), tile_width)
            out_ref[rows, cols] = out_ref[rows, cols] + vals_ref[i]

        return carry

    lax.fori_loop(0, vals_ref.shape[0], body, 0, unroll=8)


def add_tiles(ids, base, vals, tile_cols, tiles_dev):
    vmem = pl.BlockSpec(memory_space=pltpu.VMEM)
    return pl.pallas_call(
        functools.partial(_add_tiles_kernel, tile_cols, tiles_dev),
        out_shape=jax.ShapeDtypeStruct(base.shape, base.dtype),
        in_specs=[pl.BlockSpec(memory_space=pltpu.SMEM), vmem, vmem],
        out_specs=vmem,
    )(ids, base, vals)

def per_device(diag_inverse, panel, trailing, agg_vals, agg_dest, agg_tile):
    row_devices = lax.axis_size(ROW_AXES)
    local_rows, local_cols = trailing.shape
    panel_width = diag_inverse.shape[0]
    part_width = panel.shape[1]
    col_index = lax.axis_index("col")
    zh_index = lax.axis_index("zh")

    tile_rows = local_rows // TILE_ROWS
    tile_cols = local_cols // TILE_COLS
    tiles_dev = tile_rows * tile_cols
    tile_values = agg_vals.reshape(agg_vals.shape[2], agg_vals.shape[3])
    targets = agg_dest.reshape(-1)
    tile_ids = agg_tile.reshape(-1)
    matches = (targets[:, None] == jnp.arange(row_devices, dtype=jnp.int32)[None, :]).astype(
        jnp.int32
    )
    earlier = jnp.cumsum(matches, axis=0) - matches
    ranks = jnp.sum(earlier * matches, axis=1)
    position = targets * CAP + ranks
    id_lanes = jnp.broadcast_to(tile_ids.astype(jnp.float32)[:, None], (tile_ids.shape[0], TILE_COLS))
    payload = jnp.concatenate([tile_values, id_lanes], axis=1)
    send = (
        jnp.zeros((row_devices * CAP, payload.shape[1]), jnp.float32)
        .at[:, tile_values.shape[1]:]
        .set(float(tiles_dev))
        .at[position]
        .set(payload)
    )
    got = lax.all_to_all(send, ROW_AXES, split_axis=0, concat_axis=0, tiled=True)
    got_values = got[:, : tile_values.shape[1]]
    landing = got[:, tile_values.shape[1]].astype(jnp.int32)

    n_zh = lax.axis_size("zh")
    n_c = lax.axis_size("col")
    n_x = lax.axis_size("x")
    ring_panel, moved_panel = front_exchange(panel, n_x, n_zh, n_c)

    def to_rows(blocks):
        blocks = blocks.reshape(n_zh, n_c, local_rows, part_width).transpose(0, 2, 1, 3)
        return blocks.reshape(n_zh * local_rows, n_c * part_width)

    own_panel = lax.dynamic_index_in_dim(
        to_rows(ring_panel).reshape(n_zh, local_rows, panel_width), zh_index, 0, keepdims=False
    )
    own_full = jnp.dot(
        own_panel,
        diag_inverse.T,
        precision=lax.Precision.HIGHEST,
        preferred_element_type=jnp.float32,
    )
    own_block = lax.dynamic_slice_in_dim(own_full, col_index * part_width, part_width, 1)
    chosen = jnp.dot(
        to_rows(moved_panel),
        diag_inverse.T,
        precision=lax.Precision.HIGHEST,
        preferred_element_type=jnp.float32,
    ).reshape(n_zh, local_rows, panel_width)
    gathered = lax.all_gather(chosen, ("y", "core"), axis=1, tiled=False)
    partner = gathered.reshape(local_cols, panel_width)

    product = lax.dot_general(
        own_full,
        partner,
        (((1,), (1,)), ((), ())),
        precision=lax.Precision.HIGH,
        preferred_element_type=jnp.float32,
    )
    updated = add_tiles(
        landing,
        trailing - product,
        got_values.reshape(-1, TILE_ROWS, TILE_COLS),
        tile_cols,
        tiles_dev,
    )
    return (updated, own_block)


def solution(mesh):
    n_row, n_col = mesh.devices.shape
    shape = (n_col, n_col, n_col, n_row // n_col**3, n_col)
    split = Mesh(mesh.devices.reshape(shape), ROW_AXES + ("col",))
    rows = ROW_AXES
    in_specs = (
        P(),
        P(rows, "col"),
        P(rows, "col"),
        P(rows, "col", None, None),
        P(rows, "col", None, None),
        P(rows, "col", None),
    )
    out_specs = (P(rows, "col"), P(rows, "col"))
    return jax.shard_map(
        per_device, mesh=split, in_specs=in_specs, out_specs=out_specs, check_vma=False
    )
```
